256 devices in a mesh: seq: 64 (over z, x, core), head: 4 (over y).
Axes of the slice: x: 4, y: 4, z: 8, core: 2. Of those that a mesh axis runs over, the one named last changes fastest.
Arguments:
- qk: bfloat16 [65536, 2048], P('seq', 'head'), may hold values from -8 to 8
- values: bfloat16 [65536, 2048], P('seq', 'head'), may hold values from -6 to 6
- out_weight: bfloat16 [2048, 2048], P('head'), may hold values from -0.125 to 0.125
- out_cotangent: bfloat16 [65536, 2048], P('seq', 'head'), may hold values from -6 to 6
- cluster_ids: int32 [512, 16], P(None, 'head'), may hold values from 0 to 127, as said below
Outputs:
- output: bfloat16 [65536, 2048], P('seq', 'head')
- grad_qk: bfloat16 [65536, 2048], P('seq', 'head')
- grad_values: bfloat16 [65536, 2048], P('seq', 'head')
The draws below stay inside these ranges and needn't reach their ends.
Inputs may be any that keep to these rules, and one draw needn't show every extreme that they name: `cluster_ids`: call c // 2 the owner of cluster c. Over the blocks of one seq index and the heads of one head index, at most 2 name clusters of one owner, and exactly 2 for some owner. For every head, the clusters of each owner hold exactly 8 blocks together, and some cluster holds all 8.
All inputs are finite; a program needn't handle non-finite values.
Results may differ from the reference program's by a relative error of at most 0.013.
Values may be sent and summed in bfloat16 or wider, within the bound.
A program may use at most 128 MiB of HBM per device.

```python
import jax
import jax.numpy as jnp
from jax import lax

HEADS = 16
HEAD_DIM = 128
BLOCK = 128
CL_OWN = 2
BLK_DEV = 8
HD = 4
D_MODEL = 2048
NBLK = 512
TOKENS = 65536
SEND_CAP = 2
N_SEQ = 64
N_HEAD = 4


def draw_qk(key, part):
    key_a = jax.random.fold_in(key, 0)
    row_total = TOKENS
    col_total = HEADS * HEAD_DIM
    field = 1.5 * jax.random.normal(key_a, (row_total, col_total), jnp.float32)
    return jnp.clip(field, -8.0, 8.0).astype(jnp.bfloat16)


def draw_cluster_ids(key, part):
    base_key = jax.random.fold_in(key, 11)
    item_count = BLK_DEV * HD
    slot_total = N_SEQ * SEND_CAP

    def group_owners(group_key):
        key_a, key_b, key_c, key_d = jax.random.split(group_key, 4)
        relabel = jax.random.permutation(key_a, N_SEQ).astype(jnp.int32)
        ranking = jax.random.permutation(key_b, slot_total).astype(jnp.int32)
        favored = jax.random.randint(key_c, (), 0, N_SEQ, dtype=jnp.int32)
        slot_ids = jnp.arange(slot_total, dtype=jnp.int32)
        priority = jnp.where(slot_ids // SEND_CAP == favored, -1, ranking)
        picked = jnp.argsort(priority, stable=True)[:item_count].astype(jnp.int32)
        shuffle = jax.random.permutation(key_d, item_count)
        offsets = (picked // SEND_CAP)[shuffle]
        return (relabel[:, None] + offsets[None, :]) % N_SEQ
    group_keys = jax.random.split(jax.random.fold_in(base_key, 1), N_HEAD)
    owners = jax.vmap(group_owners)(group_keys)
    owners = owners.reshape(N_HEAD, N_SEQ, BLK_DEV, HD).transpose(1, 2, 0, 3).reshape(NBLK, HEADS)
    chooser = jax.random.randint(jax.random.fold_in(base_key, 2), (NBLK, HEADS), 0, 4, dtype=jnp.int32)
    head_ids = jnp.arange(HEADS, dtype=jnp.int32)
    forced = (owners == 0) & (head_ids[None, :] % HD == 0)
    second = jnp.where((chooser == 0) & jnp.logical_not(forced), 1, 0)
    return (owners * CL_OWN + second).astype(jnp.int32)


def block_levels(rng, dims, pieces, least, top_value):
    level, own = 1.0, jax.random.fold_in(rng, 6)
    for dim, blocks in pieces:
        steps = jnp.exp(jax.random.uniform(jax.random.fold_in(own, dim), (blocks,), jnp.float32, least / len(pieces), top_value / len(pieces)))
        level = level * jnp.repeat(steps, dims[dim] // blocks).reshape([-1 if axis == dim else 1 for axis in range(len(dims))])
    return level


def normal_values(stream_key, extent, deviation, limit, cuts=(), kind=jnp.bfloat16):
    result = deviation * jax.random.normal(stream_key, extent, jnp.float32)
    if cuts:
        result = result * block_levels(stream_key, extent, cuts, -0.22, 0.18)
    return jnp.clip(result, -limit, limit).astype(kind)


def setup_inputs(seed: int = 0) -> dict:
    streams_of = jax.random.split(jax.random.key(seed), 6)
    return {
        "qk": draw_qk(jax.random.fold_in(streams_of[5], 71), 0),
        "values": normal_values(streams_of[1], (TOKENS, D_MODEL), 1.0, 6.0, ((0, 64), (1, 4))),
        "out_weight": normal_values(streams_of[2], (D_MODEL, D_MODEL), D_MODEL ** -0.5, 0.125, ((0, 4),)),
        "out_cotangent": normal_values(streams_of[3], (TOKENS, D_MODEL), 1.0, 6.0, ((0, 64), (1, 4))),
        "cluster_ids": draw_cluster_ids(jax.random.fold_in(streams_of[5], 71), 0),
    }


NEG_FILL = -1e30


def unit_forward(tokens_x, tokens_v, group):
    row_count = tokens_x.shape[0]
    block_rows = row_count // group.shape[0]
    scores = jnp.dot(tokens_x, tokens_x.T, preferred_element_type=jnp.float32) * (HEAD_DIM ** -0.5)
    row_group = jnp.repeat(group, block_rows)
    position = jnp.arange(row_count)
    allowed = (row_group[:, None] == row_group[None, :]) & (position[:, None] != position[None, :])
    scores = jnp.where(allowed, scores, NEG_FILL)
    row_max = jnp.max(scores, axis=1, keepdims=True)
    raised = jnp.exp(scores - row_max)
    weights = raised / jnp.sum(raised, axis=1, keepdims=True)
    attended = jnp.dot(weights.astype(jnp.bfloat16), tokens_v, preferred_element_type=jnp.float32)
    return weights, attended


def unit_backward(tokens_x, tokens_v, grad_rows, weights, attended):
    grad_weights = jnp.dot(grad_rows, tokens_v.T, preferred_element_type=jnp.float32)
    row_delta = jnp.sum(grad_rows.astype(jnp.float32) * attended, axis=1, keepdims=True)
    grad_scores = weights * (grad_weights - row_delta)
    symmetric = (grad_scores + grad_scores.T).astype(jnp.bfloat16)
    grad_x = (jnp.dot(symmetric, tokens_x, preferred_element_type=jnp.float32) * (HEAD_DIM ** -0.5)).astype(jnp.bfloat16)
    grad_v = jnp.dot(weights.astype(jnp.bfloat16).T, grad_rows, preferred_element_type=jnp.float32).astype(jnp.bfloat16)
    return grad_x, grad_v


def by_head(array):
    return array.reshape(NBLK, BLOCK, HEADS, HEAD_DIM).transpose(2, 0, 1, 3)


def by_token(array):
    return array.transpose(1, 2, 0, 3).reshape(TOKENS, HEADS * HEAD_DIM)


def reference(qk, values, out_weight, out_cotangent, cluster_ids):
    grad_attended = jnp.dot(out_cotangent, out_weight.T, preferred_element_type=jnp.float32).astype(jnp.bfloat16)
    owners = (cluster_ids // CL_OWN).T.astype(jnp.int32)

    def one_head(operands):
        head_x, head_v, head_g, head_owner, head_group = operands
        order = jnp.argsort(head_owner, stable=True).astype(jnp.int32)
        restore = jnp.argsort(order, stable=True).astype(jnp.int32)

        def one_owner(blocks):
            tokens_x = head_x[blocks].reshape(-1, HEAD_DIM)
            tokens_v = head_v[blocks].reshape(-1, HEAD_DIM)
            grad_rows = head_g[blocks].reshape(-1, HEAD_DIM)
            weights, attended = unit_forward(tokens_x, tokens_v, head_group[blocks])
            grad_x, grad_v = unit_backward(tokens_x, tokens_v, grad_rows, weights, attended)
            return attended.astype(jnp.bfloat16), grad_x, grad_v

        first, second, third = lax.map(one_owner, order.reshape(N_SEQ, BLK_DEV))
        first = first.reshape(NBLK, BLOCK, HEAD_DIM)[restore]
        second = second.reshape(NBLK, BLOCK, HEAD_DIM)[restore]
        third = third.reshape(NBLK, BLOCK, HEAD_DIM)[restore]
        return first, second, third

    head_att, head_gx, head_gv = lax.map(one_head, (by_head(qk), by_head(values), by_head(grad_attended), owners, cluster_ids.T.astype(jnp.int32)))
    attended = by_token(head_att)
    group_cols = HD * HEAD_DIM
    total = jnp.zeros((TOKENS, D_MODEL), jnp.float32)
    for group_index in range(N_HEAD):
        att_part = attended[:, group_index * group_cols:(group_index + 1) * group_cols]
        weight_part = out_weight[group_index * group_cols:(group_index + 1) * group_cols]
        partial_term = jnp.dot(att_part, weight_part, preferred_element_type=jnp.float32).astype(jnp.bfloat16)
        total = total + lax.optimization_barrier(partial_term).astype(jnp.float32)
    return total.astype(jnp.bfloat16), by_token(head_gx), by_token(head_gv)
```

```python
import functools
import math

import jax
import jax.numpy as jnp
import numpy as np
from jax import lax
from jax.experimental import pallas as pl
from jax.experimental.pallas import tpu as pltpu
from jax.sharding import PartitionSpec as P

BLOCK = 128
CL_OWN = 2
N_SEQ = 64
SLABS = 8
COLS = 8
ITEMS = 32
HD = 4
BLK_DEV = 8
NBLK = 512
TOK = 1024
WIDTH = 512
MESH = pl.DeviceIdType.MESH
NEG = -1e30
LOG2E = math.log2(math.e)
FAST = (7, 12)
FULL = (16, 16)
VMEM_BYTES = 60 * 1024 * 1024


def placements():
    owner = np.arange(N_SEQ)
    maps = []
    for width, mults in ((1, (1,)), (2, (1, 3, 5, 7)), (4, range(1, 16, 2)), (8, range(1, 32, 2))):
        for mult in mults:
            e = (mult * owner) % N_SEQ
            slab = (e // width) % SLABS
            col = (e // (width * SLABS)) * width + e % width
            maps.append(slab * COLS + col)
    rng = np.random.RandomState(7)
    while len(maps) < 32:
        maps.append(rng.permutation(N_SEQ))
    return np.stack(maps).astype(np.int32)


PLACES = placements()


def choose_places(owners):
    lanes = jnp.arange(N_SEQ, dtype=jnp.int32)
    cnt = jnp.sum((owners[:, :, None] == lanes).astype(jnp.int32), axis=1)
    slab_of = np.zeros((N_SEQ, PLACES.shape[0] * SLABS), np.float32)
    for p in range(PLACES.shape[0]):
        slab_of[np.arange(N_SEQ), p * SLABS + PLACES[p] // COLS] = 1
    loads = jnp.dot(
        cnt.astype(jnp.bfloat16), jnp.asarray(slab_of, jnp.bfloat16), preferred_element_type=jnp.float32
    )
    worst = jnp.max(loads.reshape(N_SEQ, PLACES.shape[0], SLABS), axis=(0, 2))
    pick = jnp.argmin(worst).astype(jnp.int32)
    onehot = (jnp.arange(PLACES.shape[0], dtype=jnp.int32) == pick)[:, None]
    place = jnp.sum(jnp.where(onehot, PLACES, 0), axis=0)
    col_load = jnp.max(jnp.sum(cnt.reshape(SLABS, COLS, N_SEQ), axis=0))
    return place, jnp.min(worst), col_load


def table(hit, value):
    return jnp.sum(jnp.where(hit, value, 0), axis=-1).astype(jnp.int32)


def routing(cluster_ids, owners, place, k2, k3):
    me = lax.axis_index("seq").astype(jnp.int32)
    z_me, a_me = me // COLS, me % COLS
    lanes = jnp.arange(N_SEQ, dtype=jnp.int32)
    owner_me = jnp.sum(jnp.where(place == me, lanes, 0))
    col = lax.dynamic_index_in_dim(owners.reshape(SLABS, COLS, ITEMS), a_me, 1, keepdims=False)
    pos = jnp.sum(jnp.where(col[:, :, None] == lanes, place, 0), axis=2)
    zc, ac = pos // COLS, pos % COLS
    item = jnp.arange(ITEMS, dtype=jnp.int32)
    earlier = item[None, :] < item[:, None]
    r = jnp.sum(((zc[:, :, None] == zc[:, None, :]) & earlier).astype(jnp.int32), axis=2)
    flat = col.reshape(-1)
    order = jnp.arange(SLABS * ITEMS, dtype=jnp.int32)
    w = jnp.sum(
        ((flat[:, None] == flat[None, :]) & (order[None, :] < order[:, None])).astype(jnp.int32), axis=1
    )
    slots2 = jnp.arange(SLABS * k2, dtype=jnp.int32)[:, None]
    slots3 = jnp.arange(COLS * k3, dtype=jnp.int32)[:, None]
    zc_own = lax.dynamic_index_in_dim(zc, z_me, 0, keepdims=False)
    r_own = lax.dynamic_index_in_dim(r, z_me, 0, keepdims=False)
    out2 = zc_own * k2 + r_own
    t2 = table((r_own < k2) & (out2 == slots2), item)
    mid = (zc == z_me).reshape(-1)
    in2 = (jnp.arange(SLABS, dtype=jnp.int32)[:, None] * k2 + r).reshape(-1)
    out3 = ac.reshape(-1) * k3 + w
    t3 = table(mid & (w < k3) & (out3 == slots3), jnp.minimum(in2, SLABS * k2 - 1))
    r2 = table(mid & (r.reshape(-1) < k2) & (in2 == slots2), jnp.minimum(out3, COLS * k3 - 1))
    rf = jnp.minimum(out2, SLABS * k2 - 1)
    mine = (owners == owner_me).astype(jnp.bfloat16)
    by_col = mine.reshape(SLABS, COLS, ITEMS).transpose(1, 0, 2).reshape(COLS, SLABS * ITEMS)
    upper = jnp.asarray(np.triu(np.ones((SLABS * ITEMS, SLABS * ITEMS)), 1), jnp.bfloat16)
    wf = jnp.dot(by_col, upper, preferred_element_type=jnp.float32).astype(jnp.int32)
    by_head = mine.reshape(NBLK, HD).T
    upper = jnp.asarray(np.triu(np.ones((NBLK, NBLK)), 1), jnp.bfloat16)
    pf = jnp.dot(by_head, upper, preferred_element_type=jnp.float32).astype(jnp.int32)
    wf_head = wf.reshape(COLS, SLABS, BLK_DEV, HD).transpose(3, 1, 0, 2).reshape(HD, NBLK)
    col_head = (jnp.arange(NBLK, dtype=jnp.int32) // BLK_DEV) % COLS
    place8 = jnp.arange(BLK_DEV, dtype=jnp.int32)[None, :, None]
    chosen = (by_head[:, None, :] > 0) & (pf[:, None, :] == place8)
    tu = table(chosen, jnp.minimum(col_head * k3 + wf_head, COLS * k3 - 1)[:, None, :]).reshape(-1)
    group = table(chosen, cluster_ids.T[:, None, :])
    pf_col = pf.reshape(HD, SLABS, COLS, BLK_DEV).transpose(2, 1, 3, 0).reshape(COLS, SLABS * ITEMS)
    unit = (order % HD)[None, :] * BLK_DEV + pf_col
    r3 = table(
        (by_col[:, None, :] > 0) & (wf[:, None, :] == jnp.arange(k3, dtype=jnp.int32)[None, :, None]),
        unit[:, None, :],
    ).reshape(-1)
    tables = jnp.concatenate([t2, t3, tu, r3, r2, rf])
    same = group[:, :, None] == group[:, None, :]
    bias = jnp.where(jnp.repeat(same, BLOCK, axis=2), 0.0, NEG).astype(jnp.float32)
    return tables, bias


def exchange_kernel(n_in, n_out, k2, k3, chunks, window, order, *refs):
    tab = refs[0]
    n = n_in + n_out
    srcs = refs[1 : 1 + n]
    outs = refs[1 + n : 1 + 2 * n]
    scratch = list(refs[1 + 2 * n :])
    rows = BLOCK // chunks
    tasks = [(arr, c) for arr, c in order]
    bufs = {}
    for arr, c in tasks:
        bufs[arr, c] = tuple(scratch[:4])
        scratch = scratch[4:]
    staged = scratch.pop(0) if n_in else None
    sends, recvs, local = scratch
    me = lax.axis_index("seq")
    z_me, a_me = me // COLS, me % COLS
    t2_at = 0
    t3_at = t2_at + SLABS * k2
    tu_at = t3_at + COLS * k3
    r3_at = tu_at + ITEMS
    r2_at = r3_at + COLS * k3
    rf_at = r2_at + SLABS * k2

    def along_z(d):
        return lax.rem(z_me + d, SLABS)

    def along_a(d):
        return lax.rem(a_me + d, COLS)

    barrier = pltpu.get_barrier_semaphore()
    for d in range(1, SLABS):
        pl.semaphore_signal(barrier, inc=1, device_id={"seq": along_z(d) * COLS + a_me}, device_id_type=MESH)
    for d in range(1, COLS):
        pl.semaphore_signal(barrier, inc=1, device_id={"seq": z_me * COLS + along_a(d)}, device_id_type=MESH)
    pl.semaphore_wait(barrier, SLABS + COLS - 2)

    index = {t: i for i, t in enumerate(tasks)}

    def copies(task, stage, send_buf, recv_buf, is_z):
        size = k2 if is_z else k3
        mine = z_me if is_z else a_me
        s = index[task] * 2 + stage
        out = []
        for d in range(8):
            to = along_z(d) if is_z else along_a(d)
            src = send_buf.at[pl.ds(to * size, size)]
            dst = recv_buf.at[pl.ds(mine * size, size)]
            if d == 0:
                out.append(pltpu.make_async_copy(src, dst, local.at[s]))
            else:
                peer = to * COLS + a_me if is_z else z_me * COLS + to
                out.append(
                    pltpu.make_async_remote_copy(
                        src_ref=src,
                        dst_ref=dst,
                        send_sem=sends.at[s, d],
                        recv_sem=recvs.at[s, d],
                        device_id={"seq": peer},
                        device_id_type=MESH,
                    )
                )
        return out

    def pack(load, dst, count, base, is_z, cps):
        for d in (4, 3, 5, 2, 6, 1, 7, 0):
            to = along_z(d) if is_z else along_a(d)

            @pl.loop(0, count, unroll=True)
            def _(k):
                slot = to * count + k
                dst[slot] = load(tab[base + slot])

            cps[d].start()

    def tile(ref):
        return lambda i: ref[i]

    live = {}

    def stage1(task):
        arr, c = task
        b = bufs[task]
        if arr < n_in:
            cps = copies(task, 0, b[0], b[1], True)
            src = srcs[arr]

            for j in range(ITEMS):
                at = (j // HD) * BLOCK + c * rows
                staged[j] = src[at : at + rows, (j % HD) * BLOCK : (j % HD + 1) * BLOCK]
            pack(tile(staged), b[0], k2, t2_at, True, cps)
        else:
            cps = copies(task, 0, b[0], b[1], False)
            src = srcs[arr]

            def load(i):
                return src[i, c * rows : (c + 1) * rows, :]

            pack(load, b[0], k3, r3_at, False, cps)
        live[task, 0] = cps

    def arrive(task, stage):
        cps = live[task, stage]
        for d in range(1, 8):
            cps[d].wait_recv()
        cps[0].wait()

    def stage2(task):
        arr, c = task
        b = bufs[task]
        if arr < n_in:
            cps = copies(task, 1, b[2], b[3], False)
            pack(tile(b[1]), b[2], k3, t3_at, False, cps)
        else:
            cps = copies(task, 1, b[2], b[3], True)
            pack(tile(b[1]), b[2], k2, r2_at, True, cps)
        live[task, 1] = cps

    def stage3(task):
        arr, c = task
        load = tile(bufs[task][3])
        out = outs[arr]
        if arr < n_in:

            @pl.loop(0, ITEMS, unroll=4)
            def _(u):
                out[u, c * rows : (c + 1) * rows, :] = load(tab[tu_at + u])
        else:

            @pl.loop(0, BLK_DEV)
            def _(b):
                for h in range(HD):
                    out[pl.ds(pl.multiple_of(b * BLOCK + c * rows, rows), rows), h * BLOCK : (h + 1) * BLOCK] = load(
                        tab[rf_at + b * HD + h]
                    )

    for task in tasks[:window]:
        stage1(task)
    for i, task in enumerate(tasks):
        arrive(task, 0)
        if i + window < len(tasks):
            stage1(tasks[i + window])
        stage2(task)
        if i >= 2:
            arrive(tasks[i - 2], 1)
            stage3(tasks[i - 2])
    for task in tasks[max(0, len(tasks) - 2) :]:
        arrive(task, 1)
        stage3(task)
    for task in tasks:
        for stage in (0, 1):
            for cp in live[task, stage][1:]:
                cp.wait_send()


def exchange(tables, ins, outs, caps, chunks, window, order, cid):
    k2, k3 = caps
    n_in, n_out = len(ins), len(outs)
    rows = BLOCK // chunks
    scratch = []
    for arr, c in order:
        size2, size3 = SLABS * k2, COLS * k3
        sizes = (size2, size2, size3, size3) if arr < n_in else (size3, size3, size2, size2)
        scratch += [pltpu.VMEM((s, rows, BLOCK), jnp.bfloat16) for s in sizes]
    n_task = len(order)
    if n_in:
        scratch.append(pltpu.VMEM((ITEMS, rows, BLOCK), jnp.bfloat16))
    scratch += [
        pltpu.SemaphoreType.DMA((2 * n_task, 8)),
        pltpu.SemaphoreType.DMA((2 * n_task, 8)),
        pltpu.SemaphoreType.DMA((2 * n_task,)),
    ]
    shapes = [jax.ShapeDtypeStruct((ITEMS, BLOCK, BLOCK), jnp.bfloat16)] * n_in
    shapes += [jax.ShapeDtypeStruct((TOK, WIDTH), jnp.bfloat16)] * n_out
    vmem = pl.BlockSpec(memory_space=pltpu.VMEM)
    return pl.pallas_call(
        functools.partial(exchange_kernel, n_in, n_out, k2, k3, chunks, window, order),
        out_shape=shapes,
        in_specs=[pl.BlockSpec(memory_space=pltpu.SMEM)] + [vmem] * (n_in + n_out),
        out_specs=[vmem] * (n_in + n_out),
        scratch_shapes=scratch,
        compiler_params=pltpu.CompilerParams(
            collective_id=cid, has_side_effects=True, vmem_limit_bytes=VMEM_BYTES
        ),
        cost_estimate=pl.CostEstimate(
            flops=0, bytes_accessed=(n_in + n_out) * 100 * 1024 * 1024, transcendentals=0
        ),
    )(tables, *ins, *outs)


NT = (((1,), (1,)), ((), ()))
TN = (((0,), (0,)), ((), ()))


def mm(a, b, dims=(((1,), (0,)), ((), ()))):
    return lax.dot_general(a, b, dims, preferred_element_type=jnp.float32)


def forward_kernel(x_ref, v_ref, bias_ref, att_ref, attt_ref, lse_ref, s_ref, p_ref):
    c2 = (BLOCK ** -0.5) * LOG2E
    x = x_ref[...]
    diag = lax.broadcasted_iota(jnp.int32, (BLOCK, BLOCK), 0) == lax.broadcasted_iota(
        jnp.int32, (BLOCK, BLOCK), 1
    )
    m = jnp.full((1, TOK), NEG, jnp.float32)
    for i in range(BLK_DEV):
        at = slice(i * BLOCK, (i + 1) * BLOCK)
        s_ref[at, :] = mm(x_ref[at, :], x, NT)
        s_ref[at, at] = jnp.where(diag, NEG, s_ref[at, at])
        top = jnp.max(s_ref[at, :], axis=0, keepdims=True)
        m = jnp.maximum(m, top * c2 + bias_ref[0, i : i + 1, :])
    l = jnp.zeros((1, TOK), jnp.float32)
    for i in range(BLK_DEV):
        at = slice(i * BLOCK, (i + 1) * BLOCK)
        p = jnp.exp2(s_ref[at, :] * c2 + (bias_ref[0, i : i + 1, :] - m))
        l = l + jnp.sum(p, axis=0, keepdims=True)
        p_ref[at, :] = p.astype(jnp.bfloat16)
    attt = mm(v_ref[...], p_ref[...], TN) * (1.0 / l)
    attt_ref[0] = attt
    att_ref[...] = attt.T.astype(jnp.bfloat16)
    lse_ref[0] = jnp.broadcast_to(m + jnp.log2(l), (8, TOK))


def attention_forward(x, v, bias):
    head = pl.BlockSpec((TOK, BLOCK), lambda h: (h, 0))
    return pl.pallas_call(
        forward_kernel,
        grid=(HD,),
        in_specs=[head, head, pl.BlockSpec((1, BLK_DEV, TOK), lambda h: (h, 0, 0))],
        out_specs=[
            head,
            pl.BlockSpec((1, BLOCK, TOK), lambda h: (h, 0, 0)),
            pl.BlockSpec((1, 8, TOK), lambda h: (h, 0, 0)),
        ],
        out_shape=[
            jax.ShapeDtypeStruct((HD * TOK, BLOCK), jnp.bfloat16),
            jax.ShapeDtypeStruct((HD, BLOCK, TOK), jnp.float32),
            jax.ShapeDtypeStruct((HD, 8, TOK), jnp.float32),
        ],
        scratch_shapes=[pltpu.VMEM((TOK, TOK), jnp.float32), pltpu.VMEM((TOK, TOK), jnp.bfloat16)],
        compiler_params=pltpu.CompilerParams(vmem_limit_bytes=VMEM_BYTES),
        cost_estimate=pl.CostEstimate(flops=4 * HD * TOK * TOK * BLOCK, bytes_accessed=6 << 20, transcendentals=HD * TOK * TOK),
    )(x, v, bias)


def backward_kernel(x_ref, v_ref, g_ref, bias_ref, attt_ref, lse_ref, gx_ref, gv_ref, acc_ref, acct_ref):
    c2 = (BLOCK ** -0.5) * LOG2E
    x = x_ref[...]
    g = g_ref[...]
    diag = lax.broadcasted_iota(jnp.int32, (BLOCK, BLOCK), 0) == lax.broadcasted_iota(
        jnp.int32, (BLOCK, BLOCK), 1
    )
    delta = jnp.sum(g.astype(jnp.float32).T * attt_ref[0], axis=0, keepdims=True)
    lse = lse_ref[0, 0:1, :]
    for i in range(BLK_DEV):
        at = slice(i * BLOCK, (i + 1) * BLOCK)
        x_i = x_ref[at, :]
        p = jnp.exp2(mm(x_i, x, NT) * c2 + (bias_ref[0, i : i + 1, :] - lse))
        own = jnp.where(diag, 0.0, p[:, at])
        parts = [p[:, : i * BLOCK]] * (i > 0) + [own] + [p[:, (i + 1) * BLOCK :]] * (i < BLK_DEV - 1)
        p = jnp.concatenate(parts, axis=1)
        gs = p * (mm(v_ref[at, :], g, NT) - delta)
        gv_ref[at, :] = mm(p.astype(jnp.bfloat16), g).astype(jnp.bfloat16)
        gsb = gs.astype(jnp.bfloat16)
        acc_ref[at, :] = mm(gsb, x)
        add = mm(x_i, gsb, TN)
        if i == 0:
            acct_ref[...] = add
        else:
            acct_ref[...] += add
    gx_ref[...] = ((acc_ref[...] + acct_ref[...].T) * (BLOCK ** -0.5)).astype(jnp.bfloat16)


def attention_backward(x, v, g, bias, attt, lse):
    head = pl.BlockSpec((TOK, BLOCK), lambda h: (h, 0))
    return pl.pallas_call(
        backward_kernel,
        grid=(HD,),
        in_specs=[
            head,
            head,
            head,
            pl.BlockSpec((1, BLK_DEV, TOK), lambda h: (h, 0, 0)),
            pl.BlockSpec((1, BLOCK, TOK), lambda h: (h, 0, 0)),
            pl.BlockSpec((1, 8, TOK), lambda h: (h, 0, 0)),
        ],
        out_specs=[head, head],
        out_shape=[jax.ShapeDtypeStruct((HD * TOK, BLOCK), jnp.bfloat16)] * 2,
        scratch_shapes=[pltpu.VMEM((TOK, BLOCK), jnp.float32), pltpu.VMEM((BLOCK, TOK), jnp.float32)],
        compiler_params=pltpu.CompilerParams(vmem_limit_bytes=VMEM_BYTES),
        cost_estimate=pl.CostEstimate(flops=10 * HD * TOK * TOK * BLOCK, bytes_accessed=9 << 20, transcendentals=HD * TOK * TOK),
    )(x, v, g, bias, attt, lse)


def model_output(attended, out_weight):
    partial_term = jnp.dot(attended, out_weight, preferred_element_type=jnp.float32)
    return lax.psum_scatter(partial_term.astype(jnp.bfloat16), "head", scatter_dimension=1, tiled=True)


def cotangent_heads(out_cotangent, out_weight):
    gathered = lax.all_gather(out_cotangent, "head", axis=1, tiled=True)
    return jnp.einsum("tn,kn->tk", gathered, out_weight, preferred_element_type=jnp.float32).astype(
        jnp.bfloat16
    )


def chunked(arrays, chunks):
    return tuple((arr, c) for arr in range(arrays) for c in range(chunks))


def layer(qk, values, out_weight, grad_attended, tables, bias, caps, chunks, cid):
    heads, items = (HD * TOK, BLOCK), (ITEMS, BLOCK, BLOCK)
    x, v = exchange(tables, [qk, values], [], caps, chunks, 2, chunked(2, chunks), cid)
    x, v = x.reshape(heads), v.reshape(heads)
    att, attt, lse = attention_forward(x, v, bias)
    mixed = tuple((arr, c) for c in range(chunks) for arr in range(2))
    g, attended = exchange(tables, [grad_attended], [att.reshape(items)], caps, chunks, 4, mixed, cid + 1)
    output = model_output(attended, out_weight)
    gx, gv = attention_backward(x, v, g.reshape(heads), bias, attt, lse)
    gx, gv = gx.reshape(items), gv.reshape(items)
    grad_qk, grad_values = exchange(tables, [], [gx, gv], caps, chunks, 2, chunked(2, chunks), cid + 2)
    return output, grad_qk, grad_values


def per_device(qk, values, out_weight, out_cotangent, cluster_ids):
    owners = (cluster_ids // CL_OWN).reshape(N_SEQ, ITEMS)
    place, load2, load3 = choose_places(owners)
    tables, bias = routing(cluster_ids, owners, place, *FAST)
    over = ((load2 > FAST[0]) | (load3 > FAST[1])).astype(jnp.int32)
    over = lax.pmax(over, "head")
    grad_attended = cotangent_heads(out_cotangent, out_weight)
    fast = layer(qk, values, out_weight, grad_attended, tables, bias, FAST, 4, 0)

    def slow(args):
        tables, bias = routing(cluster_ids, owners, place, *FULL)
        return layer(qk, values, out_weight, grad_attended, tables, bias, FULL, 1, 3)

    return lax.cond(over > 0, slow, lambda args: args, fast)


def solution(mesh):
    return jax.shard_map(
        per_device,
        mesh=mesh,
        in_specs=(
            P("seq", "head"),
            P("seq", "head"),
            P("head", None),
            P("seq", "head"),
            P(None, "head"),
        ),
        out_specs=(P("seq", "head"), P("seq", "head"), P("seq", "head")),
        check_vma=False,
    )
```

```python
import functools
import math

import jax
import jax.numpy as jnp
import numpy as np
from jax import lax
from jax.experimental import pallas as pl
from jax.experimental.pallas import tpu as pltpu
from jax.sharding import PartitionSpec as P

BLOCK = 128
CL_OWN = 2
N_SEQ = 64
SLABS = 8
CHIPS = 4
ITEMS = 32
POOL = 2 * ITEMS
HD = 4
BLK_DEV = 8
NBLK = 512
TOK = 1024
WIDTH = 512
S1 = 4
I32 = jnp.int32
MESH = pl.DeviceIdType.MESH
NEG = -1e30
LOG2E = math.log2(math.e)
FAST = (5, 16)
FULL = (16, 32)
VMEM_BYTES = 60 * 1024 * 1024


def rng_(n): return jnp.arange(n,dtype=I32)
def pick(hit,value): return jnp.sum(jnp.where(hit,value,0),axis=-1).astype(I32)
def places():
    owner=np.arange(N_SEQ); maps=[]
    for width,mults in ((1,(1,)),(2,(1,3,5,7)),(4,range(1,16,2)),(8,range(1,32,2))):
        for mult in mults:
            e=(mult*owner)%N_SEQ
            maps.append((e//width)%SLABS*8+(e//(width*SLABS))*width+e%width)
    r=np.random.RandomState(7)
    while len(maps)<32: maps.append(r.permutation(N_SEQ))
    return np.stack(maps).astype(np.int32)
PLACES=places()
def choose_places(owners):
    cnt=jnp.sum((owners[:,:,None]==rng_(N_SEQ)).astype(I32),axis=1)
    slab_cnt=jnp.sum(cnt.reshape(SLABS,8,N_SEQ),axis=1)
    n=PLACES.shape[0]
    slab_of=np.zeros((N_SEQ,n*SLABS),np.float32)
    for p in range(n): slab_of[np.arange(N_SEQ),p*SLABS+PLACES[p]//8]=1
    loads=jnp.dot(slab_cnt.astype(jnp.float32),jnp.asarray(slab_of),preferred_element_type=jnp.float32,precision="highest")
    worst=jnp.max(loads.reshape(SLABS,n,SLABS),axis=(0,2))
    best=jnp.argmin(worst).astype(I32)
    return jnp.sum(jnp.where((rng_(n)==best)[:,None],PLACES,0),axis=0)
def routing(me,cluster_ids,place,k2,k3):
    owners=(cluster_ids//CL_OWN).reshape(-1)
    z_me,x_me,c_me=me//8,(me//2)%4,me%2
    cap2,cap3=2*k2,2*k3
    pos=jnp.sum(jnp.where(owners[:,None]==rng_(N_SEQ),place,0),axis=1)
    zc=(pos//8).reshape(SLABS,CHIPS,POOL)
    earlier=rng_(POOL)[None,:]<rng_(POOL)[:,None]
    r=jnp.sum(((zc[...,:,None]==zc[...,None,:])&earlier).astype(I32),axis=-1)
    to=zc[...,None]==rng_(SLABS)
    n=jnp.sum(to.astype(I32),axis=2)
    over,free=jnp.maximum(n-cap2,0),jnp.maximum(cap2-n,0)
    below=(rng_(CHIPS)[None,:]<rng_(CHIPS)[:,None]).astype(I32)
    over_at=jnp.sum(below[None,:,:,None]*over[:,None],axis=2)
    free_at=jnp.sum(below[None,:,:,None]*free[:,None],axis=2)
    extra=r>=cap2
    turn=jnp.sum(jnp.where(to,over_at[:,:,None,:],0),axis=-1)+r-cap2
    def at(v):
        return jnp.sum(jnp.where(to[:,:,:,None,:],v[:,None,None,:,:],0),axis=-1)
    f0=at(free_at)
    hit=extra[...,None]&(f0<=turn[...,None])&(turn[...,None]<f0+at(free))
    own_chip=rng_(CHIPS)[None,:,None]
    via=jnp.where(extra,pick(hit,rng_(CHIPS)),own_chip)
    k=jnp.where(extra,pick(hit,at(n)+turn[...,None]-f0),r)
    s=jnp.sum((extra[...,None,:]&(via[...,:,None]==via[...,None,:])&earlier).astype(I32),axis=-1)
    lost=jnp.any(extra&((s>=2*S1)|~jnp.any(hit,-1)))
    slab_items=CHIPS*POOL
    zf,via,k,s,extra=[v.reshape(SLABS,slab_items) for v in (zc,via,k,s,extra)]
    src=jnp.broadcast_to(own_chip,(SLABS,CHIPS,POOL)).reshape(SLABS,slab_items)
    pos=pos.reshape(SLABS,slab_items)
    xd=(pos//2)%4
    here=zf==z_me
    key=jnp.where(here,via*4+xd,-1)
    before=rng_(slab_items)[None,:]<rng_(slab_items)[:,None]
    w=jnp.sum(((key[:,:,None]==key[:,None,:])&before).astype(I32),axis=-1)
    keyed=key[...,None]==rng_(16)
    hist=jnp.sum(keyed.astype(I32),axis=1)
    upto=(rng_(SLABS)[None,:]<rng_(SLABS)[:,None]).astype(I32)
    base=jnp.sum(upto[:,:,None]*hist[None],axis=1)
    w=w+jnp.sum(jnp.where(keyed,base[:,None,:],0),axis=-1)
    full_key=(zf*CHIPS+via)*CHIPS+xd
    counts=jnp.sum((full_key.reshape(-1,1)==rng_(SLABS*CHIPS*CHIPS)).astype(I32),axis=0)
    lost=lost|(jnp.max(counts)>cap3)
    zslot=zf*k2+k%k2
    rslot=rng_(SLABS)[:,None]*k2+k%k2
    zcore=k//k2
    xslot_out=xd*k3+w%k3
    xslot_in=via*k3+w%k3
    xcore=w//k3
    s_at=(s//S1)*(CHIPS*S1)+s%S1
    row=lambda v: lax.dynamic_index_in_dim(v,z_me,0,keepdims=False)
    R=lambda m: rng_(m)[:,None]
    zf_r,via_r,k_r,s_r,ex_r,src_r,zslot_r,zcore_r,sat_r=[row(v) for v in (zf,via,k,s,extra,src,zslot,zcore,s_at)]
    q=rng_(slab_items)%POOL
    t1=pick(ex_r&(src_r==x_me)&(s_r//S1==c_me)&(via_r*S1+s_r%S1==R(CHIPS*S1)),q)
    t2=pick((via_r==x_me)&(zcore_r==c_me)&(zslot_r==R(SLABS*k2)),jnp.where(ex_r,POOL+sat_r+src_r*S1,q))
    r1=pick(ex_r&(via_r==x_me)&(s_r//S1==c_me)&(src_r*S1+s_r%S1==R(CHIPS*S1)),zcore_r*(SLABS*k2)+zslot_r)
    back=jnp.where(ex_r,2*SLABS*k2+sat_r+via_r*S1,zcore_r*(SLABS*k2)+zslot_r)
    rf=lax.dynamic_slice_in_dim(back,x_me*POOL+c_me*ITEMS,ITEMS,0)
    mid=here&(via==x_me)
    fl=lambda v: v.reshape(-1)
    t3=pick(fl(mid&(xcore==c_me))&(fl(xslot_out)==R(CHIPS*k3)),fl(zcore*(SLABS*k2)+rslot))
    r2=pick((mid&(zcore==c_me))[:,None,:]&((k%k2)[:,None,:]==rng_(k2)[None,:,None]),(xcore*(CHIPS*k3)+xslot_out)[:,None,:]).reshape(-1)
    chip_me=z_me*4+x_me
    heads=lambda v: v.reshape(NBLK,HD).T
    pos_h=heads(pos)
    both=jnp.stack([pos_h==chip_me*2,pos_h==chip_me*2+1])
    upper=jnp.asarray(np.triu(np.ones((NBLK,NBLK)),1),jnp.bfloat16)
    rank=jnp.dot(both.reshape(2*HD,NBLK).astype(jnp.bfloat16),upper,preferred_element_type=jnp.float32).astype(I32).reshape(2,HD,NBLK)
    unit=rank+BLK_DEV*rng_(HD)[None,:,None]+ITEMS*rng_(2)[:,None,None]
    unit=jnp.sum(jnp.where(both,unit,0),axis=0)
    for_chip=both[0]|both[1]
    xin_h,xcore_h=heads(xslot_in),heads(xcore)
    r3=pick((for_chip&(xcore_h==c_me)).reshape(-1)&(xin_h.reshape(-1)==R(CHIPS*k3)),unit.reshape(-1))
    mine=pos_h==me
    slot=mine[:,None,:]&((unit-c_me*ITEMS)[:,None,:]==(rng_(HD)*BLK_DEV)[:,None,None]+rng_(BLK_DEV)[None,:,None])
    tu=pick(slot,(xcore_h*(CHIPS*k3)+xin_h)[:,None,:]).reshape(-1)
    group=pick(slot,cluster_ids.T[:,None,:])
    pad=lambda v,m: jnp.clip(v,0,m)
    P2,P3=2*SLABS*k2,2*CHIPS*k3
    tables=jnp.concatenate([t1,t2,pad(t3,P2-1),pad(tu,P3-1),pad(r3,POOL-1),pad(r2,P3-1),pad(r1,P2-1),pad(rf,P2+2*CHIPS*S1-1)])
    same=group[:,:,None]==group[:,None,:]
    bias=jnp.where(jnp.repeat(same,BLOCK,axis=2),0.0,NEG).astype(jnp.float32)
    return tables,bias,lost


class Link:
    def __init__(self, tab, tasks, inbound, chunks, k2, k3, scratch):
        self.tab, self.k2, self.k3, self.rows = tab, k2, k3, BLOCK // chunks
        self.tasks, self.inbound = tasks, inbound
        self.buf = {t: scratch[7 * i : 7 * i + 7] for i, t in enumerate(tasks)}
        self.sends, self.recvs = scratch[7 * len(tasks) : 7 * len(tasks) + 2]
        self.index = {t: i for i, t in enumerate(tasks)}
        self.me = lax.axis_index("seq")
        self.z, self.x, self.c = self.me // 8, (self.me // 2) % CHIPS, self.me % 2
        sizes = [CHIPS * S1, SLABS * k2, CHIPS * k3, ITEMS, CHIPS * k3, SLABS * k2, CHIPS * S1, ITEMS]
        at = np.cumsum([0] + sizes)
        self.t1, self.t2, self.t3, self.tu, self.r3, self.r2, self.r1, self.rf = [int(v) for v in at[:-1]]
        self.live = {}

    def peer(self, axis, d):
        if axis == "z":
            to = lax.rem(self.z + d, SLABS)
            return to, to * 8 + self.x * 2 + self.c
        if axis == "x":
            to = lax.rem(self.x + d, CHIPS)
            return to, self.z * 8 + to * 2 + self.c
        return 1 - self.c, self.me + 1 - 2 * self.c

    def peers(self):
        out = [self.peer("z", d)[1] for d in range(1, SLABS)]
        out += [self.peer("x", d)[1] for d in range(1, CHIPS)]
        return out + [self.peer("c", 1)[1]]

    def barrier(self, extra=()):
        barrier = pltpu.get_barrier_semaphore()
        peers = self.peers()
        for p in peers:
            pl.semaphore_signal(barrier, inc=1, device_id={"seq": p}, device_id_type=MESH)
        for p in extra:
            pl.semaphore_signal(barrier, inc=1, device_id={"head": p}, device_id_type=MESH)
        pl.semaphore_wait(barrier, len(peers) + len(extra))

    def start(self, task, kind, d, src, dst, peer):
        s = self.index[task] * 7 + kind
        cp = pltpu.make_async_remote_copy(
            src_ref=src,
            dst_ref=dst,
            send_sem=self.sends.at[s, d],
            recv_sem=self.recvs.at[s, d],
            device_id={"seq": peer},
            device_id_type=MESH,
        )
        cp.start()
        self.live.setdefault((task, kind), []).append(cp)

    def share(self, task, kind, ref, half):
        part = ref.at[pl.ds(self.c * half, half)]
        self.start(task, kind, 0, part, part, self.peer("c", 1)[1])

    def wait(self, task, kind):
        for cp in self.live[task, kind]:
            cp.wait_recv()

    def pack(self, task, kind, axis, load, send, recv, count, base):
        n = SLABS if axis == "z" else CHIPS
        order = (4, 3, 5, 2, 6, 1, 7, 0) if axis == "z" else (2, 1, 3, 0)
        mine = self.z if axis == "z" else self.x
        at = self.c * (n * count) + mine * count
        for d in order:
            to, peer = self.peer(axis, d)

            @pl.loop(0, count, unroll=True)
            def _(k):
                tile = load(self.tab[base + to * count + k])
                if d == 0:
                    recv[at + k] = tile
                else:
                    send[to * count + k] = tile

            if d:
                self.start(task, kind, d, send.at[pl.ds(to * count, count)], recv.at[pl.ds(at, count)], peer)

    def either(self, first, second, size):
        def load(i):
            a = first[jnp.minimum(i, size - 1)]
            b = second[jnp.maximum(i - size, 0)]
            return jnp.where(i < size, a, b)

        return load

    def run(self, stage, task, src=None, out=None):
        pool, s1, arr, zs, zr, xs, xr = self.buf[task]
        k2, k3, rows = self.k2, self.k3, self.rows
        c = task[1]
        at = slice(c * rows, (c + 1) * rows)
        inward = self.inbound[task[0]]
        if stage == "A":
            if inward:
                for j in range(ITEMS):
                    b, h = j // HD, j % HD
                    pool[self.c * ITEMS + j] = src[
                        b * BLOCK + c * rows : b * BLOCK + (c + 1) * rows, h * BLOCK : (h + 1) * BLOCK
                    ]
            else:

                @pl.loop(0, ITEMS, unroll=8)
                def _(u):
                    pool[self.c * ITEMS + u] = src[u, at, :]

            self.share(task, 0, pool, ITEMS)
        elif stage == "B":
            self.wait(task, 0)
            if inward:
                self.pack(task, 1, "x", lambda i: pool[i], s1, arr, S1, self.t1)
            else:
                self.pack(task, 5, "x", lambda i: pool[i], xs, xr, k3, self.r3)
        elif stage == "C":
            if inward:
                self.wait(task, 1)
                self.share(task, 2, arr, CHIPS * S1)
            else:
                self.wait(task, 5)
                self.share(task, 6, xr, CHIPS * k3)
        elif stage == "D":
            if inward:
                self.wait(task, 2)
                self.pack(task, 3, "z", self.either(pool, arr, POOL), zs, zr, k2, self.t2)
            else:
                self.wait(task, 6)
                self.pack(task, 3, "z", lambda i: xr[i], zs, zr, k2, self.r2)
        elif stage == "E":
            self.wait(task, 3)
            self.share(task, 4, zr, SLABS * k2)
        elif stage == "F":
            self.wait(task, 4)
            if inward:
                self.pack(task, 5, "x", lambda i: zr[i], xs, xr, k3, self.t3)
            else:
                self.pack(task, 1, "x", lambda i: zr[i], s1, arr, S1, self.r1)
        elif stage == "G":
            if inward:
                self.wait(task, 5)
                self.share(task, 6, xr, CHIPS * k3)
            else:
                self.wait(task, 1)
                self.share(task, 2, arr, CHIPS * S1)
        elif stage == "H":
            if inward:
                self.wait(task, 6)

                @pl.loop(0, ITEMS, unroll=8)
                def _(u):
                    out[u, at, :] = xr[self.tab[self.tu + u]]
            else:
                self.wait(task, 2)
                load = self.either(zr, arr, 2 * SLABS * k2)

                @pl.loop(0, BLK_DEV)
                def _(b):
                    for h in range(HD):
                        out[pl.ds(pl.multiple_of(b * BLOCK + c * rows, rows), rows), h * BLOCK : (h + 1) * BLOCK] = load(
                            self.tab[self.rf + b * HD + h]
                        )

    def drain(self):
        for cps in self.live.values():
            for cp in cps:
                cp.wait_send()


def link_scratch(n_task, chunks, k2, k3):
    sizes = (POOL, CHIPS * S1, ITEMS, SLABS * k2, 2 * SLABS * k2, CHIPS * k3, 2 * CHIPS * k3)
    out = []
    for _ in range(n_task):
        out += [pltpu.VMEM((s, BLOCK // chunks, BLOCK), jnp.bfloat16) for s in sizes]
    return out + [pltpu.SemaphoreType.DMA((7 * n_task, 8))] * 2


def chunked(arrays, chunks):
    return tuple((arr, c) for arr in range(arrays) for c in range(chunks))


def stream(link, window, srcs, outs):
    tasks = link.tasks
    n = len(tasks)

    def step(stage, i):
        if 0 <= i < n:
            arr = tasks[i][0]
            link.run(stage, tasks[i], srcs[arr], outs[arr])

    for tick in range(-window - 3, n + 2):
        step("E", tick)
        step("D", tick + window)
        step("C", tick + window + 1)
        step("G", tick - 1)
        step("B", tick + window + 2)
        step("A", tick + window + 3)
        step("F", tick)
        step("H", tick - 1)


def exchange_kernel(inward, n, caps, chunks, window, flagged, *refs):
    tab, refs = refs[0], list(refs[1:])
    flag = refs.pop(0) if flagged else None
    srcs, refs = refs[:n], refs[n:]
    outs, refs = refs[:n], refs[n:]
    any_flag = refs.pop(0) if flagged else None
    if flagged:
        flags, fsend, frecv = refs[-3:]
        refs = refs[:-3]
    link = Link(tab, chunked(n, chunks), [inward] * n, chunks, *caps, refs)
    if flagged:
        y = lax.axis_index("head")
        others = [lax.rem(y + d, 4) for d in range(1, 4)]
        link.barrier(others)
        flags[y] = flag[...]
        cps = []
        for d, to in enumerate(others):
            cps.append(
                pltpu.make_async_remote_copy(
                    src_ref=flag,
                    dst_ref=flags.at[y],
                    send_sem=fsend.at[d],
                    recv_sem=frecv.at[d],
                    device_id={"head": to},
                    device_id_type=MESH,
                )
            )
            cps[-1].start()
    else:
        link.barrier()
    stream(link, window, srcs, outs)
    if flagged:
        for cp in cps:
            cp.wait()
        any_flag[...] = jnp.max(flags[...], axis=0)
    link.drain()


def exchange(tables, arrays, inward, caps, chunks, window, cid, flag=None):
    n = len(arrays)
    flagged = flag is not None
    shape = (ITEMS, BLOCK, BLOCK) if inward else (TOK, WIDTH)
    vmem = pl.BlockSpec(memory_space=pltpu.VMEM)
    scratch = link_scratch(n * chunks, chunks, *caps)
    extra_in, extra_out = [], []
    if flagged:
        extra_in = [flag]
        extra_out = [jax.ShapeDtypeStruct((8, BLOCK), jnp.float32)]
        scratch += [pltpu.VMEM((4, 8, BLOCK), jnp.float32)] + [pltpu.SemaphoreType.DMA((3,))] * 2
    return pl.pallas_call(
        functools.partial(exchange_kernel, inward, n, caps, chunks, window, flagged),
        out_shape=[jax.ShapeDtypeStruct(shape, jnp.bfloat16)] * n + extra_out,
        in_specs=[pl.BlockSpec(memory_space=pltpu.SMEM)] + [vmem] * (n + len(extra_in)),
        out_specs=[vmem] * (n + len(extra_out)),
        scratch_shapes=scratch,
        compiler_params=pltpu.CompilerParams(
            collective_id=cid, has_side_effects=True, vmem_limit_bytes=VMEM_BYTES
        ),
        cost_estimate=pl.CostEstimate(flops=0, bytes_accessed=n * 100 * 1024 * 1024, transcendentals=0),
    )(tables, *extra_in, *arrays)


NT = (((1,), (1,)), ((), ()))
TN = (((0,), (0,)), ((), ()))


def mm(a, b, dims=(((1,), (0,)), ((), ()))):
    return lax.dot_general(a, b, dims, preferred_element_type=jnp.float32)


def diagonal():
    shape = (BLOCK, BLOCK)
    return lax.broadcasted_iota(I32, shape, 0) == lax.broadcasted_iota(I32, shape, 1)


def of_head(ref, h):
    return ref[pl.ds(h * BLK_DEV, BLK_DEV)].reshape(TOK, BLOCK)


def head_forward(h, x_ref, v_ref, bias_ref, att_ref, attt_ref, lse_ref, s_ref, p_ref):
    c2 = (BLOCK ** -0.5) * LOG2E
    x = of_head(x_ref, h)
    diag = diagonal()
    m = jnp.full((1, TOK), NEG, jnp.float32)
    for i in range(BLK_DEV):
        at = slice(i * BLOCK, (i + 1) * BLOCK)
        s_ref[at, :] = mm(x[at, :], x, NT)
        s_ref[at, at] = jnp.where(diag, NEG, s_ref[at, at])
        top = jnp.max(s_ref[at, :], axis=0, keepdims=True)
        m = jnp.maximum(m, top * c2 + bias_ref[h, i : i + 1, :])
    l = jnp.zeros((1, TOK), jnp.float32)
    for i in range(BLK_DEV):
        at = slice(i * BLOCK, (i + 1) * BLOCK)
        p = jnp.exp2(s_ref[at, :] * c2 + (bias_ref[h, i : i + 1, :] - m))
        l = l + jnp.sum(p, axis=0, keepdims=True)
        p_ref[at, :] = p.astype(jnp.bfloat16)
    attt = mm(of_head(v_ref, h), p_ref[...], TN) * (1.0 / l)
    attt_ref[h] = attt
    att_ref[pl.ds(h * BLK_DEV, BLK_DEV)] = attt.T.astype(jnp.bfloat16).reshape(BLK_DEV, BLOCK, BLOCK)
    lse_ref[h] = jnp.broadcast_to(m + jnp.log2(l), (8, TOK))


def head_backward(h, x_ref, v_ref, g_ref, bias_ref, attt_ref, lse_ref, gx_ref, gv_ref, acc_ref, acct_ref):
    c2 = (BLOCK ** -0.5) * LOG2E
    x = of_head(x_ref, h)
    g = of_head(g_ref, h)
    diag = diagonal()
    delta = jnp.sum(g.astype(jnp.float32).T * attt_ref[h], axis=0, keepdims=True)
    lse = lse_ref[h, 0:1, :]
    for i in range(BLK_DEV):
        at = slice(i * BLOCK, (i + 1) * BLOCK)
        x_i = x[at, :]
        p = jnp.exp2(mm(x_i, x, NT) * c2 + (bias_ref[h, i : i + 1, :] - lse))
        own = jnp.where(diag, 0.0, p[:, at])
        parts = [p[:, : i * BLOCK]] * (i > 0) + [own] + [p[:, (i + 1) * BLOCK :]] * (i < BLK_DEV - 1)
        p = jnp.concatenate(parts, axis=1)
        gs = p * (mm(v_ref[h * BLK_DEV + i], g, NT) - delta)
        gv_ref[h * BLK_DEV + i] = mm(p.astype(jnp.bfloat16), g).astype(jnp.bfloat16)
        gsb = gs.astype(jnp.bfloat16)
        acc_ref[at, :] = mm(gsb, x)
        add = mm(x_i, gsb, TN)
        if i == 0:
            acct_ref[...] = add
        else:
            acct_ref[...] += add
    gx = (acc_ref[...] + acct_ref[...].T) * (BLOCK ** -0.5)
    gx_ref[pl.ds(h * BLK_DEV, BLK_DEV)] = gx.astype(jnp.bfloat16).reshape(BLK_DEV, BLOCK, BLOCK)


FORWARD_SCRATCH = (
    pltpu.VMEM((HD, BLOCK, TOK), jnp.float32),
    pltpu.VMEM((HD, 8, TOK), jnp.float32),
    pltpu.VMEM((TOK, TOK), jnp.float32),
    pltpu.VMEM((TOK, TOK), jnp.bfloat16),
)
BACKWARD_SCRATCH = (pltpu.VMEM((TOK, BLOCK), jnp.float32), pltpu.VMEM((BLOCK, TOK), jnp.float32))
UNITS = jax.ShapeDtypeStruct((ITEMS, BLOCK, BLOCK), jnp.bfloat16)
TOKENS = jax.ShapeDtypeStruct((TOK, WIDTH), jnp.bfloat16)


def middle_kernel(caps, chunks, tab, g_src, x_ref, v_ref, bias_ref, attended, gx_ref, gv_ref, *scratch):
    scratch = list(scratch)
    attt, lse, s_ref, p_ref, acc, acct, att, g_ref = scratch[:8]
    tasks = chunked(2, chunks)
    link = Link(tab, tasks, [True, False], chunks, *caps, scratch[8:])
    link.barrier()
    ins = [(0, c) for c in range(chunks)]
    homes = [(1, c) for c in range(chunks)]
    for stage in "ABCD":
        for t in ins:
            link.run(stage, t, g_src)

    @pl.loop(0, HD)
    def _(h):
        head_forward(h, x_ref, v_ref, bias_ref, att, attt, lse, s_ref, p_ref)

    for t in homes:
        link.run("A", t, att)
    for t in homes:
        link.run("B", t)
    for c in range(chunks):
        link.run("E", ins[c])
        link.run("C", homes[c])
        link.run("F", ins[c])
        link.run("D", homes[c])
    for t in ins:
        link.run("G", t)
    for t in ins:
        link.run("H", t, None, g_ref)

    @pl.loop(0, HD)
    def _(h):
        head_backward(h, x_ref, v_ref, g_ref, bias_ref, attt, lse, gx_ref, gv_ref, acc, acct)

    for stage in "EFGH":
        for t in homes:
            link.run(stage, t, None, attended)
    link.drain()


def middle(tables, grad_attended, x, v, bias, caps, chunks, cid):
    vmem = pl.BlockSpec(memory_space=pltpu.VMEM)
    units = pltpu.VMEM((ITEMS, BLOCK, BLOCK), jnp.bfloat16)
    return pl.pallas_call(
        functools.partial(middle_kernel, caps, chunks),
        out_shape=[TOKENS, UNITS, UNITS],
        in_specs=[pl.BlockSpec(memory_space=pltpu.SMEM)] + [vmem] * 4,
        out_specs=[vmem] * 3,
        scratch_shapes=list(FORWARD_SCRATCH + BACKWARD_SCRATCH) + [units, units] + link_scratch(2 * chunks, chunks, *caps),
        compiler_params=pltpu.CompilerParams(
            collective_id=cid, has_side_effects=True, vmem_limit_bytes=VMEM_BYTES
        ),
        cost_estimate=pl.CostEstimate(flops=14 * HD * TOK * TOK * BLOCK, bytes_accessed=200 * 1024 * 1024, transcendentals=0),
    )(tables, grad_attended, x, v, bias)


def attention_kernel(x_ref, v_ref, g_ref, bias_ref, att, gx_ref, gv_ref, attt, lse, s_ref, p_ref, acc, acct):
    @pl.loop(0, HD)
    def _(h):
        head_forward(h, x_ref, v_ref, bias_ref, att, attt, lse, s_ref, p_ref)
        head_backward(h, x_ref, v_ref, g_ref, bias_ref, attt, lse, gx_ref, gv_ref, acc, acct)


def attention(x, v, g, bias):
    vmem = pl.BlockSpec(memory_space=pltpu.VMEM)
    return pl.pallas_call(
        attention_kernel,
        out_shape=[UNITS] * 3,
        in_specs=[vmem] * 4,
        out_specs=[vmem] * 3,
        scratch_shapes=list(FORWARD_SCRATCH + BACKWARD_SCRATCH),
        compiler_params=pltpu.CompilerParams(vmem_limit_bytes=VMEM_BYTES),
    )(x, v, g, bias)


def model_output(attended, out_weight):
    partial_term = jnp.dot(attended, out_weight, preferred_element_type=jnp.float32)
    return lax.psum_scatter(partial_term.astype(jnp.bfloat16), "head", scatter_dimension=1, tiled=True)


def cotangent_heads(out_cotangent, out_weight):
    gathered = lax.all_gather(out_cotangent, "head", axis=1, tiled=True)
    return jnp.einsum("tn,kn->tk", gathered, out_weight, preferred_element_type=jnp.float32).astype(
        jnp.bfloat16
    )


def per_device(qk, values, out_weight, out_cotangent, cluster_ids):
    me = lax.axis_index("seq").astype(I32)
    place = choose_places((cluster_ids // CL_OWN).reshape(N_SEQ, ITEMS))
    tables, bias, lost = routing(me, cluster_ids, place, *FAST)
    flag = jnp.broadcast_to(lost.astype(jnp.float32), (8, BLOCK))
    grad_attended = cotangent_heads(out_cotangent, out_weight)
    x, v, any_lost = exchange(tables, [qk, values], True, FAST, 4, 2, 0, flag)
    attended, gx, gv = middle(tables, grad_attended, x, v, bias, FAST, 4, 1)
    output = model_output(attended, out_weight)
    grad_qk, grad_values = exchange(tables, [gx, gv], False, FAST, 4, 2, 2)

    def slow(args):
        tables, bias, _ = routing(me, cluster_ids, place, *FULL)
        sources = jnp.stack([qk, values, grad_attended])
        x, v, g = lax.map(lambda a: exchange(tables, [a], True, FULL, 1, 1, 3)[0], sources)
        units = jnp.stack(attention(x, v, g, bias))
        home = lax.map(lambda a: exchange(tables, [a], False, FULL, 1, 1, 4)[0], units)
        return model_output(home[0], out_weight), home[1], home[2]

    return lax.cond(any_lost[0, 0] > 0, slow, lambda args: args, (output, grad_qk, grad_values))


def solution(mesh):
    return jax.shard_map(
        per_device,
        mesh=mesh,
        in_specs=(
            P("seq", "head"),
            P("seq", "head"),
            P("head", None),
            P("seq", "head"),
            P(None, "head"),
        ),
        out_specs=(P("seq", "head"), P("seq", "head"), P("seq", "head")),
        check_vma=False,
    )
```

```python
import functools
import math

import jax
import jax.numpy as jnp
import numpy as np
from jax import lax
from jax.experimental import pallas as pl
from jax.experimental.pallas import tpu as pltpu
from jax.sharding import PartitionSpec as P

BLOCK = 128
CL_OWN = 2
N_SEQ = 64
SLABS = 8
CHIPS = 4
ITEMS = 32
POOL = 2 * ITEMS
HD = 4
BLK_DEV = 8
NBLK = 512
TOK = 1024
WIDTH = 512
S1 = 4
I32 = jnp.int32
MESH = pl.DeviceIdType.MESH
NEG = -1e30
LOG2E = math.log2(math.e)
FAST = (5, 15)
FULL = (16, 32)
VMEM_BYTES = 60 * 1024 * 1024


def rng_(n): return jnp.arange(n,dtype=I32)
def pick(hit,value): return jnp.sum(jnp.where(hit,value,0),axis=-1).astype(I32)
def places():
    owner=np.arange(N_SEQ); maps=[]
    for width,mults in ((1,(1,)),(2,(1,3,5,7)),(4,range(1,16,2)),(8,range(1,32,2))):
        for mult in mults:
            e=(mult*owner)%N_SEQ
            maps.append((e//width)%SLABS*8+(e//(width*SLABS))*width+e%width)
    r=np.random.RandomState(7)
    while len(maps)<32: maps.append(r.permutation(N_SEQ))
    return np.stack(maps).astype(np.int32)
PLACES=places()
def choose_places(owners):
    cnt=jnp.sum((owners[:,:,None]==rng_(N_SEQ)).astype(I32),axis=1)
    slab_cnt=jnp.sum(cnt.reshape(SLABS,8,N_SEQ),axis=1)
    n=PLACES.shape[0]
    slab_of=np.zeros((N_SEQ,n*SLABS),np.float32)
    for p in range(n): slab_of[np.arange(N_SEQ),p*SLABS+PLACES[p]//8]=1
    loads=jnp.dot(slab_cnt.astype(jnp.float32),jnp.asarray(slab_of),preferred_element_type=jnp.float32,precision="highest")
    worst=jnp.max(loads.reshape(SLABS,n,SLABS),axis=(0,2))
    best=jnp.argmin(worst).astype(I32)
    return jnp.sum(jnp.where((rng_(n)==best)[:,None],PLACES,0),axis=0)
def routing(me,cluster_ids,place,k2,k3):
    owners=(cluster_ids//CL_OWN).reshape(-1)
    z_me,x_me,c_me=me//8,(me//2)%4,me%2
    cap2,cap3=2*k2,2*k3
    pos=jnp.sum(jnp.where(owners[:,None]==rng_(N_SEQ),place,0),axis=1)
    zc=(pos//8).reshape(SLABS,CHIPS,POOL)
    earlier=rng_(POOL)[None,:]<rng_(POOL)[:,None]
    r=jnp.sum(((zc[...,:,None]==zc[...,None,:])&earlier).astype(I32),axis=-1)
    to=zc[...,None]==rng_(SLABS)
    n=jnp.sum(to.astype(I32),axis=2)
    over,free=jnp.maximum(n-cap2,0),jnp.maximum(cap2-n,0)
    below=(rng_(CHIPS)[None,:]<rng_(CHIPS)[:,None]).astype(I32)
    over_at=jnp.sum(below[None,:,:,None]*over[:,None],axis=2)
    free_at=jnp.sum(below[None,:,:,None]*free[:,None],axis=2)
    extra=r>=cap2
    turn=jnp.sum(jnp.where(to,over_at[:,:,None,:],0),axis=-1)+r-cap2
    def at(v):
        return jnp.sum(jnp.where(to[:,:,:,None,:],v[:,None,None,:,:],0),axis=-1)
    f0=at(free_at)
    hit=extra[...,None]&(f0<=turn[...,None])&(turn[...,None]<f0+at(free))
    own_chip=rng_(CHIPS)[None,:,None]
    via=jnp.where(extra,pick(hit,rng_(CHIPS)),own_chip)
    k=jnp.where(extra,pick(hit,at(n)+turn[...,None]-f0),r)
    s=jnp.sum((extra[...,None,:]&(via[...,:,None]==via[...,None,:])&earlier).astype(I32),axis=-1)
    lost=jnp.any(extra&((s>=2*S1)|~jnp.any(hit,-1)))
    slab_items=CHIPS*POOL
    zf,via,k,s,extra=[v.reshape(SLABS,slab_items) for v in (zc,via,k,s,extra)]
    src=jnp.broadcast_to(own_chip,(SLABS,CHIPS,POOL)).reshape(SLABS,slab_items)
    pos=pos.reshape(SLABS,slab_items)
    xd=(pos//2)%4
    here=zf==z_me
    key=jnp.where(here,via*4+xd,-1)
    before=rng_(slab_items)[None,:]<rng_(slab_items)[:,None]
    w=jnp.sum(((key[:,:,None]==key[:,None,:])&before).astype(I32),axis=-1)
    keyed=key[...,None]==rng_(16)
    hist=jnp.sum(keyed.astype(I32),axis=1)
    upto=(rng_(SLABS)[None,:]<rng_(SLABS)[:,None]).astype(I32)
    base=jnp.sum(upto[:,:,None]*hist[None],axis=1)
    w=w+jnp.sum(jnp.where(keyed,base[:,None,:],0),axis=-1)
    full_key=(zf*CHIPS+via)*CHIPS+xd
    counts=jnp.sum((full_key.reshape(-1,1)==rng_(SLABS*CHIPS*CHIPS)).astype(I32),axis=0)
    lost=lost|(jnp.max(counts)>cap3)
    zslot=zf*k2+k%k2
    rslot=rng_(SLABS)[:,None]*k2+k%k2
    zcore=k//k2
    xslot_out=xd*k3+w%k3
    xslot_in=via*k3+w%k3
    xcore=w//k3
    s_at=(s//S1)*(CHIPS*S1)+s%S1
    row=lambda v: lax.dynamic_index_in_dim(v,z_me,0,keepdims=False)
    R=lambda m: rng_(m)[:,None]
    zf_r,via_r,k_r,s_r,ex_r,src_r,zslot_r,zcore_r,sat_r=[row(v) for v in (zf,via,k,s,extra,src,zslot,zcore,s_at)]
    q=rng_(slab_items)%POOL
    t1=pick(ex_r&(src_r==x_me)&(s_r//S1==c_me)&(via_r*S1+s_r%S1==R(CHIPS*S1)),q)
    t2=pick((via_r==x_me)&(zcore_r==c_me)&(zslot_r==R(SLABS*k2)),jnp.where(ex_r,POOL+sat_r+src_r*S1,q))
    r1=pick(ex_r&(via_r==x_me)&(s_r//S1==c_me)&(src_r*S1+s_r%S1==R(CHIPS*S1)),zcore_r*(SLABS*k2)+zslot_r)
    back=jnp.where(ex_r,2*SLABS*k2+sat_r+via_r*S1,zcore_r*(SLABS*k2)+zslot_r)
    rf=lax.dynamic_slice_in_dim(back,x_me*POOL+c_me*ITEMS,ITEMS,0)
    mid=here&(via==x_me)
    fl=lambda v: v.reshape(-1)
    t3=pick(fl(mid&(xcore==c_me))&(fl(xslot_out)==R(CHIPS*k3)),fl(zcore*(SLABS*k2)+rslot))
    r2=pick((mid&(zcore==c_me))[:,None,:]&((k%k2)[:,None,:]==rng_(k2)[None,:,None]),(xcore*(CHIPS*k3)+xslot_out)[:,None,:]).reshape(-1)
    chip_me=z_me*4+x_me
    heads=lambda v: v.reshape(NBLK,HD).T
    pos_h=heads(pos)
    both=jnp.stack([pos_h==chip_me*2,pos_h==chip_me*2+1])
    upper=jnp.asarray(np.triu(np.ones((NBLK,NBLK)),1),jnp.bfloat16)
    rank=jnp.dot(both.reshape(2*HD,NBLK).astype(jnp.bfloat16),upper,preferred_element_type=jnp.float32).astype(I32).reshape(2,HD,NBLK)
    unit=rank+BLK_DEV*rng_(HD)[None,:,None]+ITEMS*rng_(2)[:,None,None]
    unit=jnp.sum(jnp.where(both,unit,0),axis=0)
    for_chip=both[0]|both[1]
    xin_h,xcore_h=heads(xslot_in),heads(xcore)
    r3=pick((for_chip&(xcore_h==c_me)).reshape(-1)&(xin_h.reshape(-1)==R(CHIPS*k3)),unit.reshape(-1))
    mine=pos_h==me
    slot=mine[:,None,:]&((unit-c_me*ITEMS)[:,None,:]==(rng_(HD)*BLK_DEV)[:,None,None]+rng_(BLK_DEV)[None,:,None])
    tu=pick(slot,(xcore_h*(CHIPS*k3)+xin_h)[:,None,:]).reshape(-1)
    group=pick(slot,cluster_ids.T[:,None,:])
    pad=lambda v,m: jnp.clip(v,0,m)
    P2,P3=2*SLABS*k2,2*CHIPS*k3
    tables=jnp.concatenate([t1,t2,pad(t3,P2-1),pad(tu,P3-1),pad(r3,POOL-1),pad(r2,P3-1),pad(r1,P2-1),pad(rf,P2+2*CHIPS*S1-1)])
    same=group[:,:,None]==group[:,None,:]
    bias=jnp.where(jnp.repeat(same,BLOCK,axis=2),0.0,NEG).astype(jnp.float32)
    return tables,bias,lost


class Link:
    def __init__(self, tab, tasks, inbound, chunks, k2, k3, scratch, sets):
        self.tab, self.k2, self.k3, self.rows = tab, k2, k3, BLOCK // chunks
        self.tasks, self.inbound = tasks, inbound
        self.buf = {t: scratch[7 * (i % sets) : 7 * (i % sets) + 7] for i, t in enumerate(tasks)}
        self.sends, self.recvs = scratch[7 * sets : 7 * sets + 2]
        self.index = {t: i % sets for i, t in enumerate(tasks)}
        self.me = lax.axis_index("seq")
        self.z, self.x, self.c = self.me // 8, (self.me // 2) % CHIPS, self.me % 2
        sizes = [CHIPS * S1, SLABS * k2, CHIPS * k3, ITEMS, CHIPS * k3, SLABS * k2, CHIPS * S1, ITEMS]
        at = np.cumsum([0] + sizes)
        self.t1, self.t2, self.t3, self.tu, self.r3, self.r2, self.r1, self.rf = [int(v) for v in at[:-1]]
        self.live = {}

    def peer(self, axis, d):
        if axis == "z":
            to = lax.rem(self.z + d, SLABS)
            return to, to * 8 + self.x * 2 + self.c
        if axis == "x":
            to = lax.rem(self.x + d, CHIPS)
            return to, self.z * 8 + to * 2 + self.c
        return 1 - self.c, self.me + 1 - 2 * self.c

    def peers(self):
        out = [self.peer("z", d)[1] for d in range(1, SLABS)]
        out += [self.peer("x", d)[1] for d in range(1, CHIPS)]
        return out + [self.peer("c", 1)[1]]

    def barrier(self, extra=()):
        barrier = pltpu.get_barrier_semaphore()
        peers = self.peers()
        for p in peers:
            pl.semaphore_signal(barrier, inc=1, device_id={"seq": p}, device_id_type=MESH)
        for p in extra:
            pl.semaphore_signal(barrier, inc=1, device_id={"head": p}, device_id_type=MESH)
        pl.semaphore_wait(barrier, len(peers) + len(extra))

    def start(self, task, kind, d, src, dst, peer):
        s = self.index[task] * 7 + kind
        cp = pltpu.make_async_remote_copy(
            src_ref=src,
            dst_ref=dst,
            send_sem=self.sends.at[s, d],
            recv_sem=self.recvs.at[s, d],
            device_id={"seq": peer},
            device_id_type=MESH,
        )
        cp.start()
        self.live.setdefault((task, kind), []).append(cp)

    def share(self, task, kind, ref, half):
        part = ref.at[pl.ds(self.c * half, half)]
        self.start(task, kind, 0, part, part, self.peer("c", 1)[1])

    def wait(self, task, kind):
        for cp in self.live[task, kind]:
            cp.wait_recv()

    def sent(self, task, *kinds):
        for kind in kinds:
            for cp in self.live.pop((task, kind)):
                cp.wait_send()

    def pack(self, task, kind, axis, load, send, recv, count, base):
        n = SLABS if axis == "z" else CHIPS
        order = (4, 3, 5, 2, 6, 1, 7, 0) if axis == "z" else (2, 1, 3, 0)
        mine = self.z if axis == "z" else self.x
        at = self.c * (n * count) + mine * count
        for d in order:
            to, peer = self.peer(axis, d)

            @pl.loop(0, count, unroll=True)
            def _(k):
                tile = load(self.tab[base + to * count + k])
                if d == 0:
                    recv[at + k] = tile
                else:
                    send[to * count + k] = tile

            if d:
                self.start(task, kind, d, send.at[pl.ds(to * count, count)], recv.at[pl.ds(at, count)], peer)

    def either(self, first, second, size):
        def load(i):
            a = first[jnp.minimum(i, size - 1)]
            b = second[jnp.maximum(i - size, 0)]
            return jnp.where(i < size, a, b)

        return load

    def run(self, stage, task, src=None, out=None):
        pool, s1, arr, zs, zr, xs, xr = self.buf[task]
        k2, k3, rows = self.k2, self.k3, self.rows
        c = task[1]
        at = slice(c * rows, (c + 1) * rows)
        inward = self.inbound[task[0]]
        if stage == "A":
            if inward:
                for j in range(ITEMS):
                    b, h = j // HD, j % HD
                    pool[self.c * ITEMS + j] = src[
                        b * BLOCK + c * rows : b * BLOCK + (c + 1) * rows, h * BLOCK : (h + 1) * BLOCK
                    ]
            else:

                @pl.loop(0, ITEMS, unroll=8)
                def _(u):
                    pool[self.c * ITEMS + u] = src[u, at, :]

            self.share(task, 0, pool, ITEMS)
        elif stage == "B":
            self.wait(task, 0)
            if inward:
                self.pack(task, 1, "x", lambda i: pool[i], s1, arr, S1, self.t1)
            else:
                self.pack(task, 5, "x", lambda i: pool[i], xs, xr, k3, self.r3)
        elif stage == "C":
            if inward:
                self.wait(task, 1)
                self.share(task, 2, arr, CHIPS * S1)
            else:
                self.wait(task, 5)
                self.share(task, 6, xr, CHIPS * k3)
        elif stage == "D":
            if inward:
                self.wait(task, 2)
                self.sent(task, 0, 1, 2)
                self.pack(task, 3, "z", self.either(pool, arr, POOL), zs, zr, k2, self.t2)
            else:
                self.wait(task, 6)
                self.sent(task, 0, 5, 6)
                self.pack(task, 3, "z", lambda i: xr[i], zs, zr, k2, self.r2)
        elif stage == "E":
            self.wait(task, 3)
            self.share(task, 4, zr, SLABS * k2)
        elif stage == "F":
            self.wait(task, 4)
            self.sent(task, 3, 4)
            if inward:
                self.pack(task, 5, "x", lambda i: zr[i], xs, xr, k3, self.t3)
            else:
                self.pack(task, 1, "x", lambda i: zr[i], s1, arr, S1, self.r1)
        elif stage == "G":
            if inward:
                self.wait(task, 5)
                self.share(task, 6, xr, CHIPS * k3)
            else:
                self.wait(task, 1)
                self.share(task, 2, arr, CHIPS * S1)
        elif stage == "H":
            if inward:
                self.wait(task, 6)
                self.sent(task, 5, 6)

                @pl.loop(0, ITEMS, unroll=8)
                def _(u):
                    out[u, at, :] = xr[self.tab[self.tu + u]]
            else:
                self.wait(task, 2)
                self.sent(task, 1, 2)
                load = self.either(zr, arr, 2 * SLABS * k2)

                @pl.loop(0, BLK_DEV)
                def _(b):
                    for h in range(HD):
                        out[pl.ds(pl.multiple_of(b * BLOCK + c * rows, rows), rows), h * BLOCK : (h + 1) * BLOCK] = load(
                            self.tab[self.rf + b * HD + h]
                        )


def link_scratch(sets, chunks, k2, k3):
    sizes = (POOL, CHIPS * S1, ITEMS, SLABS * k2, 2 * SLABS * k2, CHIPS * k3, 2 * CHIPS * k3)
    out = []
    for _ in range(sets):
        out += [pltpu.VMEM((s, BLOCK // chunks, BLOCK), jnp.bfloat16) for s in sizes]
    return out + [pltpu.SemaphoreType.DMA((7 * sets, 8))] * 2


def chunked(arrays, chunks):
    return tuple((arr, c) for arr in range(arrays) for c in range(chunks))


def exchange_kernel(inward, caps, tab, src, out, *scratch):
    task = (0, 0)
    link = Link(tab, [task], [inward], 1, *caps, scratch, 1)
    link.barrier()
    for stage in "ABCDEFGH":
        link.run(stage, task, src, out)


def exchange(tables, array, inward, caps, cid):
    vmem = pl.BlockSpec(memory_space=pltpu.VMEM)
    return pl.pallas_call(
        functools.partial(exchange_kernel, inward, caps),
        out_shape=UNITS if inward else TOKENS,
        in_specs=[pl.BlockSpec(memory_space=pltpu.SMEM), vmem],
        out_specs=vmem,
        scratch_shapes=link_scratch(1, 1, *caps),
        compiler_params=pltpu.CompilerParams(
            collective_id=cid, has_side_effects=True, vmem_limit_bytes=VMEM_BYTES
        ),
    )(tables, array)


NT = (((1,), (1,)), ((), ()))
TN = (((0,), (0,)), ((), ()))


def mm(a, b, dims=(((1,), (0,)), ((), ()))):
    return lax.dot_general(a, b, dims, preferred_element_type=jnp.float32)


def diagonal():
    shape = (BLOCK, BLOCK)
    return lax.broadcasted_iota(I32, shape, 0) == lax.broadcasted_iota(I32, shape, 1)


def of_head(ref, h):
    return ref[pl.ds(h * BLK_DEV, BLK_DEV)].reshape(TOK, BLOCK)


def head_forward(h, x_ref, v_ref, bias_ref, att_ref, attt_ref, lse_ref, s_ref, p_ref):
    c2 = (BLOCK ** -0.5) * LOG2E
    x = of_head(x_ref, h)
    diag = diagonal()
    m = jnp.full((1, TOK), NEG, jnp.float32)
    for i in range(BLK_DEV):
        at = slice(i * BLOCK, (i + 1) * BLOCK)
        s_ref[at, :] = mm(x[at, :], x, NT)
        s_ref[at, at] = jnp.where(diag, NEG, s_ref[at, at])
        top = jnp.max(s_ref[at, :], axis=0, keepdims=True)
        m = jnp.maximum(m, top * c2 + bias_ref[h, i : i + 1, :])
    l = jnp.zeros((1, TOK), jnp.float32)
    for i in range(BLK_DEV):
        at = slice(i * BLOCK, (i + 1) * BLOCK)
        p = jnp.exp2(s_ref[at, :] * c2 + (bias_ref[h, i : i + 1, :] - m))
        l = l + jnp.sum(p, axis=0, keepdims=True)
        p_ref[at, :] = p.astype(jnp.bfloat16)
    attt = mm(of_head(v_ref, h), p_ref[...], TN) * (1.0 / l)
    attt_ref[h] = attt
    att_ref[pl.ds(h * BLK_DEV, BLK_DEV)] = attt.T.astype(jnp.bfloat16).reshape(BLK_DEV, BLOCK, BLOCK)
    lse_ref[h] = jnp.broadcast_to(m + jnp.log2(l), (8, TOK))


def head_backward(h, x_ref, v_ref, g_ref, bias_ref, attt_ref, lse_ref, gx_ref, gv_ref, acc_ref, acct_ref):
    c2 = (BLOCK ** -0.5) * LOG2E
    x = of_head(x_ref, h)
    g = of_head(g_ref, h)
    diag = diagonal()
    delta = jnp.sum(g.astype(jnp.float32).T * attt_ref[h], axis=0, keepdims=True)
    lse = lse_ref[h, 0:1, :]
    for i in range(BLK_DEV):
        at = slice(i * BLOCK, (i + 1) * BLOCK)
        x_i = x[at, :]
        p = jnp.exp2(mm(x_i, x, NT) * c2 + (bias_ref[h, i : i + 1, :] - lse))
        own = jnp.where(diag, 0.0, p[:, at])
        parts = [p[:, : i * BLOCK]] * (i > 0) + [own] + [p[:, (i + 1) * BLOCK :]] * (i < BLK_DEV - 1)
        p = jnp.concatenate(parts, axis=1)
        gs = p * (mm(v_ref[h * BLK_DEV + i], g, NT) - delta)
        gv_ref[h * BLK_DEV + i] = mm(p.astype(jnp.bfloat16), g).astype(jnp.bfloat16)
        gsb = gs.astype(jnp.bfloat16)
        acc_ref[at, :] = mm(gsb, x)
        add = mm(x_i, gsb, TN)
        if i == 0:
            acct_ref[...] = add
        else:
            acct_ref[...] += add
    gx = (acc_ref[...] + acct_ref[...].T) * (BLOCK ** -0.5)
    gx_ref[pl.ds(h * BLK_DEV, BLK_DEV)] = gx.astype(jnp.bfloat16).reshape(BLK_DEV, BLOCK, BLOCK)


FORWARD_SCRATCH = (
    pltpu.VMEM((HD, BLOCK, TOK), jnp.float32),
    pltpu.VMEM((HD, 8, TOK), jnp.float32),
    pltpu.VMEM((TOK, TOK), jnp.float32),
    pltpu.VMEM((TOK, TOK), jnp.bfloat16),
)
BACKWARD_SCRATCH = (pltpu.VMEM((TOK, BLOCK), jnp.float32), pltpu.VMEM((BLOCK, TOK), jnp.float32))
UNITS = jax.ShapeDtypeStruct((ITEMS, BLOCK, BLOCK), jnp.bfloat16)
TOKENS = jax.ShapeDtypeStruct((TOK, WIDTH), jnp.bfloat16)


CHUNKS = 4
SETS = 8
ROWS = 256


class Heads:
    def __init__(self, sems):
        self.y = lax.axis_index("head")
        self.others = [lax.rem(self.y + d, 4) for d in range(1, 4)]
        self.sends, self.recvs = sems

    def copy(self, kind, d, src, dst):
        return pltpu.make_async_remote_copy(
            src_ref=src,
            dst_ref=dst,
            send_sem=self.sends.at[kind, d],
            recv_sem=self.recvs.at[kind, d],
            device_id={"head": self.others[d]},
            device_id_type=MESH,
        )

    def columns(self, y):
        return pl.ds(pl.multiple_of(y * WIDTH, WIDTH), WIDTH)


def layer_kernel(caps, tab, flag, qk, values, cot, weight, bias, output, grad_qk, grad_values, any_flag, *scratch):
    scratch = list(scratch)
    attt, lse, s_ref, p_ref, acc, acct = scratch[:6]
    x_u, v_u, g_u, att_u, gv_u, tokens, parts_in, parts_out, flags = scratch[6:15]
    heads = Heads(scratch[15:17])
    ready = scratch[17]
    gx_u = att_u
    tasks = chunked(6, CHUNKS)
    link = Link(tab, tasks, [True] * 3 + [False] * 3, CHUNKS, *caps, scratch[18:], SETS)
    srcs = (qk, values, tokens, att_u, gx_u, gv_u)
    outs = (x_u, v_u, g_u, tokens, grad_qk, grad_values)
    link.barrier(heads.others)

    def step(stages, *which):
        for i in which:
            for stage in stages:
                if 0 <= i < len(tasks):
                    arr = tasks[i][0]
                    link.run(stage, tasks[i], srcs[arr], outs[arr])

    def each(stage, which):
        for i in which:
            step(stage, i)

    flags[heads.y] = flag[...]
    flag_cps = [heads.copy(0, d, flag, flags.at[heads.y]) for d in range(3)]
    cot_cps = [heads.copy(1, d, cot, parts_in.at[heads.y]) for d in range(3)]

    def tick(t):
        step("H", t - 2)
        step("E", t)
        if t + 2 < 8:
            step("D", t + 2)
        if t + 3 < 8:
            step("C", t + 3)
        if t + 4 < 8:
            step("B", t + 4)
        if t + 5 < 8:
            step("A", t + 5)
        step("F", t)
        step("G", t - 1)

    tick(-5)
    for cp in flag_cps + [cot_cps[1], cot_cps[0], cot_cps[2]]:
        cp.start()
    for t in range(-4, 7):
        tick(t)

    for cp in cot_cps:
        cp.wait()

    @pl.loop(0, TOK // ROWS)
    def _(r):
        at = pl.ds(pl.multiple_of(r * ROWS, ROWS), ROWS)
        total = mm(cot[at, :], weight[:, heads.columns(heads.y)], NT)
        for other in heads.others:
            total += mm(parts_in[other, at, :], weight[:, heads.columns(other)], NT)
        tokens[at, :] = total.astype(jnp.bfloat16)

    for other in heads.others:
        pl.semaphore_signal(ready, inc=1, device_id={"head": other}, device_id_type=MESH)

    each("A", range(8, 12))
    each("B", range(8, 12))
    step("CD", 8)
    step("H", 5)
    step("E", 7)
    step("CD", 9)
    step("F", 7)
    step("G", 6)
    step("CD", 10)
    step("H", 6)
    step("E", 8)
    step("CD", 11)
    step("F", 8)
    step("G", 7)
    step("H", 7)
    step("E", 9)
    step("F", 9)
    step("G", 8)

    @pl.loop(0, HD)
    def _(h):
        head_forward(h, x_u, v_u, bias, att_u, attt, lse, s_ref, p_ref)

    each("A", range(12, 16))
    each("B", range(12, 15))
    step("H", 8)
    step("E", 10)
    step("CD", 12)
    step("F", 10)
    step("G", 9)
    step("B", 15)
    step("CD", 13)
    step("H", 9)
    step("E", 11)
    step("CD", 14)
    step("F", 11)
    step("G", 10)
    step("CD", 15)
    step("H", 10)
    step("E", 12)
    step("G", 11)
    step("F", 12)
    step("H", 11)
    step("E", 13)
    step("F", 13)
    step("G", 12)

    @pl.loop(0, HD)
    def _(h):
        head_backward(h, x_u, v_u, g_u, bias, attt, lse, gx_u, gv_u, acc, acct)

    each("A", range(16, 20))
    step("G", 13)
    each("B", range(16, 20))
    step("H", 12)
    step("E", 14)
    step("CD", 16)
    step("F", 14)
    step("CD", 17)
    step("H", 13)
    step("E", 15)
    step("CD", 18)
    step("F", 15)
    step("G", 14)
    step("CD", 19)
    step("A", 20)
    sums = [heads.copy(2, d, parts_out.at[d], parts_in.at[heads.y]) for d in range(3)]
    for t in range(16, 26):
        step("H", t - 2)
        step("E", t)
        step("D", t + 2 if t >= 18 else -1)
        step("C", t + 3 if t >= 17 else -1)
        step("B", t + 4)
        step("A", t + 5)
        step("F", t)
        step("G", t - 1)
        if t == 17:
            pl.semaphore_wait(ready, 3)
            for d in (1, 0, 2):

                @pl.loop(0, TOK // ROWS)
                def _(r):
                    at = pl.ds(pl.multiple_of(r * ROWS, ROWS), ROWS)
                    part = mm(tokens[at, :], weight[:, heads.columns(heads.others[d])])
                    parts_out[d, at, :] = part.astype(jnp.bfloat16)

                sums[d].start()

            @pl.loop(0, TOK // ROWS)
            def _(r):
                at = pl.ds(pl.multiple_of(r * ROWS, ROWS), ROWS)
                output[at, :] = mm(tokens[at, :], weight[:, heads.columns(heads.y)]).astype(jnp.bfloat16)

    for cp in flag_cps + sums:
        cp.wait()
    any_flag[...] = jnp.max(flags[...], axis=0)

    @pl.loop(0, TOK // ROWS)
    def _(r):
        at = pl.ds(pl.multiple_of(r * ROWS, ROWS), ROWS)
        total = output[at, :].astype(jnp.float32)
        for other in heads.others:
            total += parts_in[other, at, :].astype(jnp.float32)
        output[at, :] = total.astype(jnp.bfloat16)


def layer(tables, flag, qk, values, cot, weight, bias, caps, cid):
    vmem = pl.BlockSpec(memory_space=pltpu.VMEM)
    units = pltpu.VMEM((ITEMS, BLOCK, BLOCK), jnp.bfloat16)
    tokens = pltpu.VMEM((TOK, WIDTH), jnp.bfloat16)
    scratch = list(FORWARD_SCRATCH + BACKWARD_SCRATCH) + [units] * 5 + [tokens]
    scratch += [
        pltpu.VMEM((4, TOK, WIDTH), jnp.bfloat16),
        pltpu.VMEM((3, TOK, WIDTH), jnp.bfloat16),
        pltpu.VMEM((4, 8, BLOCK), jnp.float32),
        pltpu.SemaphoreType.DMA((3, 3)),
        pltpu.SemaphoreType.DMA((3, 3)),
        pltpu.SemaphoreType.REGULAR,
    ]
    return pl.pallas_call(
        functools.partial(layer_kernel, caps),
        out_shape=[TOKENS] * 3 + [jax.ShapeDtypeStruct((8, BLOCK), jnp.float32)],
        in_specs=[pl.BlockSpec(memory_space=pltpu.SMEM)] + [vmem] * 6,
        out_specs=[vmem] * 4,
        scratch_shapes=scratch + link_scratch(SETS, CHUNKS, *caps),
        compiler_params=pltpu.CompilerParams(
            collective_id=cid, has_side_effects=True, vmem_limit_bytes=VMEM_BYTES
        ),
    )(tables, flag, qk, values, cot, weight, bias)


def attention_kernel(x_ref, v_ref, g_ref, bias_ref, att, gx_ref, gv_ref, attt, lse, s_ref, p_ref, acc, acct):
    @pl.loop(0, HD)
    def _(h):
        head_forward(h, x_ref, v_ref, bias_ref, att, attt, lse, s_ref, p_ref)
        head_backward(h, x_ref, v_ref, g_ref, bias_ref, attt, lse, gx_ref, gv_ref, acc, acct)


def attention(x, v, g, bias):
    vmem = pl.BlockSpec(memory_space=pltpu.VMEM)
    return pl.pallas_call(
        attention_kernel,
        out_shape=[UNITS] * 3,
        in_specs=[vmem] * 4,
        out_specs=[vmem] * 3,
        scratch_shapes=list(FORWARD_SCRATCH + BACKWARD_SCRATCH),
        compiler_params=pltpu.CompilerParams(vmem_limit_bytes=VMEM_BYTES),
    )(x, v, g, bias)


def model_output(attended, out_weight):
    partial_term = jnp.dot(attended, out_weight, preferred_element_type=jnp.float32)
    return lax.psum_scatter(partial_term.astype(jnp.bfloat16), "head", scatter_dimension=1, tiled=True)


def cotangent_heads(out_cotangent, out_weight):
    gathered = lax.all_gather(out_cotangent, "head", axis=1, tiled=True)
    return jnp.einsum("tn,kn->tk", gathered, out_weight, preferred_element_type=jnp.float32).astype(
        jnp.bfloat16
    )


def per_device(qk, values, out_weight, out_cotangent, cluster_ids):
    me = lax.axis_index("seq").astype(I32)
    place = choose_places((cluster_ids // CL_OWN).reshape(N_SEQ, ITEMS))
    tables, bias, lost = routing(me, cluster_ids, place, *FAST)
    flag = jnp.broadcast_to(lost.astype(jnp.float32), (8, BLOCK))
    *fast, any_lost = layer(tables, flag, qk, values, out_cotangent, out_weight, bias, FAST, 0)

    def slow(args):
        tables, bias, _ = routing(me, cluster_ids, place, *FULL)
        grad_attended = cotangent_heads(out_cotangent, out_weight)
        sources = jnp.stack([qk, values, grad_attended])
        x, v, g = lax.map(lambda a: exchange(tables, a, True, FULL, 1), sources)
        units = jnp.stack(attention(x, v, g, bias))
        home = lax.map(lambda a: exchange(tables, a, False, FULL, 2), units)
        return [model_output(home[0], out_weight), home[1], home[2]]

    return tuple(lax.cond(any_lost[0, 0] > 0, slow, lambda args: args, fast))


def solution(mesh):
    return jax.shard_map(
        per_device,
        mesh=mesh,
        in_specs=(
            P("seq", "head"),
            P("seq", "head"),
            P("head", None),
            P("seq", "head"),
            P(None, "head"),
        ),
        out_specs=(P("seq", "head"), P("seq", "head"), P("seq", "head")),
        check_vma=False,
    )
```

```python
import functools
import math

import jax
import jax.numpy as jnp
import numpy as np
from jax import lax
from jax.experimental import pallas as pl
from jax.experimental.pallas import tpu as pltpu
from jax.sharding import PartitionSpec as P

BLOCK = 128
CL_OWN = 2
N_SEQ = 64
SLABS = 8
CHIPS = 4
ITEMS = 32
POOL = 2 * ITEMS
HD = 4
BLK_DEV = 8
NBLK = 512
TOK = 1024
WIDTH = 512
S1 = 4
I32 = jnp.int32
MESH = pl.DeviceIdType.MESH
NEG = -1e30
LOG2E = math.log2(math.e)
FAST = (5, 15)
FULL = (16, 32)
VMEM_BYTES = 60 * 1024 * 1024


def rng_(n): return jnp.arange(n,dtype=I32)
def pick(hit,value): return jnp.sum(jnp.where(hit,value,0),axis=-1).astype(I32)
def places():
    owner=np.arange(N_SEQ); maps=[]
    for width,mults in ((1,(1,)),(2,(1,3,5,7)),(4,range(1,16,2)),(8,range(1,32,2))):
        for mult in mults:
            e=(mult*owner)%N_SEQ
            maps.append((e//width)%SLABS*8+(e//(width*SLABS))*width+e%width)
    r=np.random.RandomState(7)
    while len(maps)<32: maps.append(r.permutation(N_SEQ))
    return np.stack(maps).astype(np.int32)
PLACES=places()
def choose_places(owners):
    cnt=jnp.sum((owners[:,:,None]==rng_(N_SEQ)).astype(I32),axis=1)
    slab_cnt=jnp.sum(cnt.reshape(SLABS,8,N_SEQ),axis=1)
    n=PLACES.shape[0]
    slab_of=np.zeros((N_SEQ,n*SLABS),np.float32)
    for p in range(n): slab_of[np.arange(N_SEQ),p*SLABS+PLACES[p]//8]=1
    loads=jnp.dot(slab_cnt.astype(jnp.float32),jnp.asarray(slab_of),preferred_element_type=jnp.float32,precision="highest")
    worst=jnp.max(loads.reshape(SLABS,n,SLABS),axis=(0,2))
    best=jnp.argmin(worst).astype(I32)
    return jnp.sum(jnp.where((rng_(n)==best)[:,None],PLACES,0),axis=0)
def routing(me,cluster_ids,place,k2,k3):
    owners=(cluster_ids//CL_OWN).reshape(-1)
    z_me,x_me,c_me=me//8,(me//2)%4,me%2
    cap2,cap3=2*k2,2*k3
    pos=jnp.sum(jnp.where(owners[:,None]==rng_(N_SEQ),place,0),axis=1)
    zc=(pos//8).reshape(SLABS,CHIPS,POOL)
    earlier=rng_(POOL)[None,:]<rng_(POOL)[:,None]
    r=jnp.sum(((zc[...,:,None]==zc[...,None,:])&earlier).astype(I32),axis=-1)
    to=zc[...,None]==rng_(SLABS)
    n=jnp.sum(to.astype(I32),axis=2)
    over,free=jnp.maximum(n-cap2,0),jnp.maximum(cap2-n,0)
    below=(rng_(CHIPS)[None,:]<rng_(CHIPS)[:,None]).astype(I32)
    over_at=jnp.sum(below[None,:,:,None]*over[:,None],axis=2)
    free_at=jnp.sum(below[None,:,:,None]*free[:,None],axis=2)
    extra=r>=cap2
    turn=jnp.sum(jnp.where(to,over_at[:,:,None,:],0),axis=-1)+r-cap2
    def at(v):
        return jnp.sum(jnp.where(to[:,:,:,None,:],v[:,None,None,:,:],0),axis=-1)
    f0=at(free_at)
    hit=extra[...,None]&(f0<=turn[...,None])&(turn[...,None]<f0+at(free))
    own_chip=rng_(CHIPS)[None,:,None]
    via=jnp.where(extra,pick(hit,rng_(CHIPS)),own_chip)
    k=jnp.where(extra,pick(hit,at(n)+turn[...,None]-f0),r)
    s=jnp.sum((extra[...,None,:]&(via[...,:,None]==via[...,None,:])&earlier).astype(I32),axis=-1)
    lost=jnp.any(extra&((s>=2*S1)|~jnp.any(hit,-1)))
    slab_items=CHIPS*POOL
    zf,via,k,s,extra=[v.reshape(SLABS,slab_items) for v in (zc,via,k,s,extra)]
    src=jnp.broadcast_to(own_chip,(SLABS,CHIPS,POOL)).reshape(SLABS,slab_items)
    pos=pos.reshape(SLABS,slab_items)
    xd=(pos//2)%4
    here=zf==z_me
    key=jnp.where(here,via*4+xd,-1)
    before=rng_(slab_items)[None,:]<rng_(slab_items)[:,None]
    w=jnp.sum(((key[:,:,None]==key[:,None,:])&before).astype(I32),axis=-1)
    keyed=key[...,None]==rng_(16)
    hist=jnp.sum(keyed.astype(I32),axis=1)
    upto=(rng_(SLABS)[None,:]<rng_(SLABS)[:,None]).astype(I32)
    base=jnp.sum(upto[:,:,None]*hist[None],axis=1)
    w=w+jnp.sum(jnp.where(keyed,base[:,None,:],0),axis=-1)
    full_key=(zf*CHIPS+via)*CHIPS+xd
    counts=jnp.sum((full_key.reshape(-1,1)==rng_(SLABS*CHIPS*CHIPS)).astype(I32),axis=0)
    lost=lost|(jnp.max(counts)>cap3)
    zslot=zf*k2+k%k2
    rslot=rng_(SLABS)[:,None]*k2+k%k2
    zcore=k//k2
    xslot_out=xd*k3+w%k3
    xslot_in=via*k3+w%k3
    xcore=w//k3
    s_at=(s//S1)*(CHIPS*S1)+s%S1
    row=lambda v: lax.dynamic_index_in_dim(v,z_me,0,keepdims=False)
    R=lambda m: rng_(m)[:,None]
    zf_r,via_r,k_r,s_r,ex_r,src_r,zslot_r,zcore_r,sat_r=[row(v) for v in (zf,via,k,s,extra,src,zslot,zcore,s_at)]
    q=rng_(slab_items)%POOL
    t1=pick(ex_r&(src_r==x_me)&(s_r//S1==c_me)&(via_r*S1+s_r%S1==R(CHIPS*S1)),q)
    t2=pick((via_r==x_me)&(zcore_r==c_me)&(zslot_r==R(SLABS*k2)),jnp.where(ex_r,POOL+sat_r+src_r*S1,q))
    r1=pick(ex_r&(via_r==x_me)&(s_r//S1==c_me)&(src_r*S1+s_r%S1==R(CHIPS*S1)),zcore_r*(SLABS*k2)+zslot_r)
    back=jnp.where(ex_r,2*SLABS*k2+sat_r+via_r*S1,zcore_r*(SLABS*k2)+zslot_r)
    rf=lax.dynamic_slice_in_dim(back,x_me*POOL+c_me*ITEMS,ITEMS,0)
    mid=here&(via==x_me)
    fl=lambda v: v.reshape(-1)
    t3=pick(fl(mid&(xcore==c_me))&(fl(xslot_out)==R(CHIPS*k3)),fl(zcore*(SLABS*k2)+rslot))
    r2=pick((mid&(zcore==c_me))[:,None,:]&((k%k2)[:,None,:]==rng_(k2)[None,:,None]),(xcore*(CHIPS*k3)+xslot_out)[:,None,:]).reshape(-1)
    chip_me=z_me*4+x_me
    heads=lambda v: v.reshape(NBLK,HD).T
    pos_h=heads(pos)
    both=jnp.stack([pos_h==chip_me*2,pos_h==chip_me*2+1])
    upper=jnp.asarray(np.triu(np.ones((NBLK,NBLK)),1),jnp.bfloat16)
    rank=jnp.dot(both.reshape(2*HD,NBLK).astype(jnp.bfloat16),upper,preferred_element_type=jnp.float32).astype(I32).reshape(2,HD,NBLK)
    unit=rank+BLK_DEV*rng_(HD)[None,:,None]+ITEMS*rng_(2)[:,None,None]
    unit=jnp.sum(jnp.where(both,unit,0),axis=0)
    for_chip=both[0]|both[1]
    xin_h,xcore_h=heads(xslot_in),heads(xcore)
    r3=pick((for_chip&(xcore_h==c_me)).reshape(-1)&(xin_h.reshape(-1)==R(CHIPS*k3)),unit.reshape(-1))
    mine=pos_h==me
    slot=mine[:,None,:]&((unit-c_me*ITEMS)[:,None,:]==(rng_(HD)*BLK_DEV)[:,None,None]+rng_(BLK_DEV)[None,:,None])
    tu=pick(slot,(xcore_h*(CHIPS*k3)+xin_h)[:,None,:]).reshape(-1)
    group=pick(slot,cluster_ids.T[:,None,:])
    pad=lambda v,m: jnp.clip(v,0,m)
    P2,P3=2*SLABS*k2,2*CHIPS*k3
    tables=jnp.concatenate([t1,t2,pad(t3,P2-1),pad(tu,P3-1),pad(r3,POOL-1),pad(r2,P3-1),pad(r1,P2-1),pad(rf,P2+2*CHIPS*S1-1)])
    same=group[:,:,None]==group[:,None,:]
    bias=jnp.where(jnp.repeat(same,BLOCK,axis=2),0.0,NEG).astype(jnp.float32)
    return tables,bias,lost


class Link:
    def __init__(self, tab, tasks, inbound, chunks, k2, k3, scratch, sets):
        self.tab, self.k2, self.k3, self.rows = tab, k2, k3, BLOCK // chunks
        self.tasks, self.inbound = tasks, inbound
        self.buf = {t: scratch[7 * (i % sets) : 7 * (i % sets) + 7] for i, t in enumerate(tasks)}
        self.sends, self.recvs = scratch[7 * sets : 7 * sets + 2]
        self.index = {t: i % sets for i, t in enumerate(tasks)}
        self.me = lax.axis_index("seq")
        self.z, self.x, self.c = self.me // 8, (self.me // 2) % CHIPS, self.me % 2
        self.t1, self.t2, self.t3, self.tu, self.r3, self.r2, self.r1, self.rf = table_offsets(k2, k3)[0]
        self.live = {}

    def peer(self, axis, d):
        if axis == "z":
            to = lax.rem(self.z + d, SLABS)
            return to, to * 8 + self.x * 2 + self.c
        if axis == "x":
            to = lax.rem(self.x + d, CHIPS)
            return to, self.z * 8 + to * 2 + self.c
        return 1 - self.c, self.me + 1 - 2 * self.c

    def peers(self):
        out = [self.peer("z", d)[1] for d in range(1, SLABS)]
        out += [self.peer("x", d)[1] for d in range(1, CHIPS)]
        return out + [self.peer("c", 1)[1]]

    def barrier(self, extra=()):
        barrier = pltpu.get_barrier_semaphore()
        peers = self.peers()
        for p in peers:
            pl.semaphore_signal(barrier, inc=1, device_id={"seq": p}, device_id_type=MESH)
        for p in extra:
            pl.semaphore_signal(barrier, inc=1, device_id={"head": p}, device_id_type=MESH)
        pl.semaphore_wait(barrier, len(peers) + len(extra))

    def start(self, task, kind, d, src, dst, peer):
        s = self.index[task] * 7 + kind
        cp = pltpu.make_async_remote_copy(
            src_ref=src,
            dst_ref=dst,
            send_sem=self.sends.at[s, d],
            recv_sem=self.recvs.at[s, d],
            device_id={"seq": peer},
            device_id_type=MESH,
        )
        cp.start()
        self.live.setdefault((task, kind), []).append(cp)

    def share(self, task, kind, ref, half):
        part = ref.at[pl.ds(self.c * half, half)]
        self.start(task, kind, 0, part, part, self.peer("c", 1)[1])

    def wait(self, task, kind):
        for cp in self.live[task, kind]:
            cp.wait_recv()

    def sent(self, task, *kinds):
        for kind in kinds:
            for cp in self.live.pop((task, kind)):
                cp.wait_send()

    def pack(self, task, kind, axis, load, send, recv, count, base):
        n = SLABS if axis == "z" else CHIPS
        order = (4, 3, 5, 2, 6, 1, 7, 0) if axis == "z" else (2, 1, 3, 0)
        mine = self.z if axis == "z" else self.x
        at = self.c * (n * count) + mine * count
        for d in order:
            to, peer = self.peer(axis, d)

            @pl.loop(0, count, unroll=True)
            def _(k):
                tile = load(self.tab[0, base + to * count + k])
                if d == 0:
                    recv[at + k] = tile
                else:
                    send[to * count + k] = tile

            if d:
                self.start(task, kind, d, send.at[pl.ds(to * count, count)], recv.at[pl.ds(at, count)], peer)

    def either(self, first, second, size):
        def load(i):
            a = first[jnp.minimum(i, size - 1)]
            b = second[jnp.maximum(i - size, 0)]
            return jnp.where(i < size, a, b)

        return load

    def run(self, stage, task, src=None, out=None):
        pool, s1, arr, zs, zr, xs, xr = self.buf[task]
        k2, k3, rows = self.k2, self.k3, self.rows
        c = task[1]
        at = slice(c * rows, (c + 1) * rows)
        inward = self.inbound[task[0]]
        if stage == "A":
            if inward:
                for j in range(ITEMS):
                    b, h = j // HD, j % HD
                    pool[self.c * ITEMS + j] = src[
                        b * BLOCK + c * rows : b * BLOCK + (c + 1) * rows, h * BLOCK : (h + 1) * BLOCK
                    ]
            else:

                @pl.loop(0, ITEMS, unroll=8)
                def _(u):
                    pool[self.c * ITEMS + u] = src[u, at, :]

            self.share(task, 0, pool, ITEMS)
        elif stage == "B":
            self.wait(task, 0)
            if inward:
                self.pack(task, 1, "x", lambda i: pool[i], s1, arr, S1, self.t1)
            else:
                self.pack(task, 5, "x", lambda i: pool[i], xs, xr, k3, self.r3)
        elif stage == "C":
            if inward:
                self.wait(task, 1)
                self.share(task, 2, arr, CHIPS * S1)
            else:
                self.wait(task, 5)
                self.share(task, 6, xr, CHIPS * k3)
        elif stage == "D":
            if inward:
                self.wait(task, 2)
                self.sent(task, 0, 1, 2)
                self.pack(task, 3, "z", self.either(pool, arr, POOL), zs, zr, k2, self.t2)
            else:
                self.wait(task, 6)
                self.sent(task, 0, 5, 6)
                self.pack(task, 3, "z", lambda i: xr[i], zs, zr, k2, self.r2)
        elif stage == "E":
            self.wait(task, 3)
            self.share(task, 4, zr, SLABS * k2)
        elif stage == "F":
            self.wait(task, 4)
            self.sent(task, 3, 4)
            if inward:
                self.pack(task, 5, "x", lambda i: zr[i], xs, xr, k3, self.t3)
            else:
                self.pack(task, 1, "x", lambda i: zr[i], s1, arr, S1, self.r1)
        elif stage == "G":
            if inward:
                self.wait(task, 5)
                self.share(task, 6, xr, CHIPS * k3)
            else:
                self.wait(task, 1)
                self.share(task, 2, arr, CHIPS * S1)
        elif stage == "H":
            if inward:
                self.wait(task, 6)
                self.sent(task, 5, 6)

                @pl.loop(0, ITEMS, unroll=8)
                def _(u):
                    out[u, at, :] = xr[self.tab[0, self.tu + u]]
            else:
                self.wait(task, 2)
                self.sent(task, 1, 2)
                load = self.either(zr, arr, 2 * SLABS * k2)

                @pl.loop(0, BLK_DEV)
                def _(b):
                    for h in range(HD):
                        out[pl.ds(pl.multiple_of(b * BLOCK + c * rows, rows), rows), h * BLOCK : (h + 1) * BLOCK] = load(
                            self.tab[0, self.rf + b * HD + h]
                        )


def link_scratch(sets, chunks, k2, k3):
    sizes = (POOL, CHIPS * S1, ITEMS, SLABS * k2, 2 * SLABS * k2, CHIPS * k3, 2 * CHIPS * k3)
    out = []
    for _ in range(sets):
        out += [pltpu.VMEM((s, BLOCK // chunks, BLOCK), jnp.bfloat16) for s in sizes]
    return out + [pltpu.SemaphoreType.DMA((7 * sets, 8))] * 2


def chunked(arrays, chunks):
    return tuple((arr, c) for arr in range(arrays) for c in range(chunks))


def exchange_kernel(inward, caps, tab, src, out, *scratch):
    task = (0, 0)
    link = Link(tab, [task], [inward], 1, *caps, scratch, 1)
    link.barrier()
    for stage in "ABCDEFGH":
        link.run(stage, task, src, out)


def exchange(tables, array, inward, caps, cid):
    vmem = pl.BlockSpec(memory_space=pltpu.VMEM)
    return pl.pallas_call(
        functools.partial(exchange_kernel, inward, caps),
        out_shape=UNITS if inward else TOKENS,
        in_specs=[pl.BlockSpec(memory_space=pltpu.SMEM), vmem],
        out_specs=vmem,
        scratch_shapes=link_scratch(1, 1, *caps),
        compiler_params=pltpu.CompilerParams(
            collective_id=cid, has_side_effects=True, vmem_limit_bytes=VMEM_BYTES
        ),
    )(tables, array)


NT = (((1,), (1,)), ((), ()))
TN = (((0,), (0,)), ((), ()))


def mm(a, b, dims=(((1,), (0,)), ((), ()))):
    return lax.dot_general(a, b, dims, preferred_element_type=jnp.float32)


def diagonal():
    shape = (BLOCK, BLOCK)
    return lax.broadcasted_iota(I32, shape, 0) == lax.broadcasted_iota(I32, shape, 1)


def of_head(ref, h):
    return ref[pl.ds(h * BLK_DEV, BLK_DEV)].reshape(TOK, BLOCK)


def head_forward(h, x_ref, v_ref, bias_ref, att_ref, attt_ref, lse_ref, s_ref, p_ref):
    c2 = (BLOCK ** -0.5) * LOG2E
    x = of_head(x_ref, h)
    diag = diagonal()
    m = jnp.full((1, TOK), NEG, jnp.float32)
    for i in range(BLK_DEV):
        at = slice(i * BLOCK, (i + 1) * BLOCK)
        s_ref[at, :] = mm(x[at, :], x, NT)
        s_ref[at, at] = jnp.where(diag, NEG, s_ref[at, at])
        top = jnp.max(s_ref[at, :], axis=0, keepdims=True)
        m = jnp.maximum(m, top * c2 + bias_ref[h, i : i + 1, :])
    l = jnp.zeros((1, TOK), jnp.float32)
    for i in range(BLK_DEV):
        at = slice(i * BLOCK, (i + 1) * BLOCK)
        p = jnp.exp2(s_ref[at, :] * c2 + (bias_ref[h, i : i + 1, :] - m))
        l = l + jnp.sum(p, axis=0, keepdims=True)
        p_ref[at, :] = p.astype(jnp.bfloat16)
    attt = mm(of_head(v_ref, h), p_ref[...], TN) * (1.0 / l)
    attt_ref[h] = attt
    att_ref[pl.ds(h * BLK_DEV, BLK_DEV)] = attt.T.astype(jnp.bfloat16).reshape(BLK_DEV, BLOCK, BLOCK)
    lse_ref[h] = jnp.broadcast_to(m + jnp.log2(l), (8, TOK))


def head_backward(h, x_ref, v_ref, g_ref, bias_ref, attt_ref, lse_ref, gx_ref, gv_ref, acc_ref, acct_ref):
    c2 = (BLOCK ** -0.5) * LOG2E
    x = of_head(x_ref, h)
    g = of_head(g_ref, h)
    diag = diagonal()
    delta = jnp.sum(g.astype(jnp.float32).T * attt_ref[h], axis=0, keepdims=True)
    lse = lse_ref[h, 0:1, :]
    for i in range(BLK_DEV):
        at = slice(i * BLOCK, (i + 1) * BLOCK)
        x_i = x[at, :]
        p = jnp.exp2(mm(x_i, x, NT) * c2 + (bias_ref[h, i : i + 1, :] - lse))
        own = jnp.where(diag, 0.0, p[:, at])
        parts = [p[:, : i * BLOCK]] * (i > 0) + [own] + [p[:, (i + 1) * BLOCK :]] * (i < BLK_DEV - 1)
        p = jnp.concatenate(parts, axis=1)
        gs = p * (mm(v_ref[h * BLK_DEV + i], g, NT) - delta)
        gv_ref[h * BLK_DEV + i] = mm(p.astype(jnp.bfloat16), g).astype(jnp.bfloat16)
        gsb = gs.astype(jnp.bfloat16)
        acc_ref[at, :] = mm(gsb, x)
        add = mm(x_i, gsb, TN)
        if i == 0:
            acct_ref[...] = add
        else:
            acct_ref[...] += add
    gx = (acc_ref[...] + acct_ref[...].T) * (BLOCK ** -0.5)
    gx_ref[pl.ds(h * BLK_DEV, BLK_DEV)] = gx.astype(jnp.bfloat16).reshape(BLK_DEV, BLOCK, BLOCK)


ROWS_R = 16
PAD = 512


def place_consts():
    n = PLACES.shape[0]
    slab_of = np.zeros((n * SLABS, N_SEQ), np.float32)
    for p in range(n):
        slab_of[p * SLABS + PLACES[p] // 8, np.arange(N_SEQ)] = 1
    pos = np.zeros((N_SEQ, BLOCK), np.float32)
    pos[:, :n] = PLACES.T
    return slab_of, pos


def table_offsets(k2, k3):
    at, out = 0, []
    for size in (CHIPS * S1, SLABS * k2, CHIPS * k3, ITEMS, CHIPS * k3, SLABS * k2, CHIPS * S1, ITEMS):
        out.append(at)
        at += -(-size // 8) * 8
    return out, at


def routing_kernel(caps, me, ids_ref, slab_of_ref, places_ref, tab_ref, bias_ref, flag_ref, pos_ref):
    k2, k3 = caps
    cap2, cap3 = 2 * k2, 2 * k3
    f32, bf16 = jnp.float32, jnp.bfloat16
    if me is None:
        me = lax.axis_index("seq")
    z_me, x_me, c_me = me // 8, (me // 2) % CHIPS, me % 2
    iota = lambda shape, axis: lax.broadcasted_iota(I32, shape, axis)
    item = (ROWS_R, 1, BLOCK)
    row, lane = iota(item, 0), iota(item, 2)
    ids = ids_ref[...]
    owner = ids // CL_OWN
    own_iota = iota((N_SEQ, BLOCK), 0)
    ll = (iota((BLOCK, BLOCK), 0), iota((BLOCK, BLOCK), 1))
    cnt = jnp.zeros((N_SEQ, BLOCK), f32)
    for z in range(SLABS):
        both = (own_iota == owner[2 * z]).astype(f32) + (own_iota == owner[2 * z + 1]).astype(f32)
        cnt += mm(both.astype(bf16), (ll[1] == z).astype(f32).astype(bf16))
    loads = mm(slab_of_ref[...].astype(bf16), cnt.astype(bf16))
    n_place = slab_of_ref.shape[0] // SLABS
    worst = jnp.max(jnp.max(loads.reshape(n_place, SLABS, BLOCK), axis=1), axis=1, keepdims=True)
    best = jnp.min(worst.astype(I32) * 64 + iota((n_place, 1), 0)) % 64
    chosen = jnp.where(iota((N_SEQ, BLOCK), 1) == best, places_ref[...], 0.0)
    place = jnp.sum(chosen, axis=1, keepdims=True)
    for r in range(ROWS_R):
        pos_ref[r] = jnp.sum(jnp.where(own_iota == owner[r], place, 0.0), axis=0, keepdims=True).astype(I32)
    pos = pos_ref[...]
    zc, xd, cd = pos // 8, (pos // 2) % CHIPS, pos % 2
    half = lane // POOL
    x = (row % 2) * 2 + half
    slab = row // 2
    q = lane % POOL
    same_half = (ll[0] // POOL) == (ll[1] // POOL)
    upper = ll[0] < ll[1]
    as_bf = lambda m: m.astype(f32).astype(bf16)

    def times(hot, matrix):
        n = hot.shape[1]
        return mm(hot.reshape(ROWS_R * n, BLOCK).astype(bf16), as_bf(matrix)).astype(I32).reshape(ROWS_R, n, BLOCK)

    def down(hot, value):
        return jnp.sum(jnp.where(hot, value, 0), axis=1, keepdims=True)

    eight = (ROWS_R, 8, BLOCK)
    sub = iota(eight, 1)
    to = sub == zc
    to_f = to.astype(f32)
    rank = times(to_f, same_half & upper)
    first, second = times(to_f, ll[0] < POOL), times(to_f, ll[0] >= POOL)

    def of_slab(v, which):
        v = v.reshape(SLABS, 2, 8, BLOCK)[:, which : which + 1]
        return jnp.concatenate([v, v], axis=1).reshape(eight)

    n = [of_slab(first, 0), of_slab(second, 0), of_slab(first, 1), of_slab(second, 1)]
    over_at = jnp.zeros(eight, I32)
    for m in range(CHIPS):
        over_at += jnp.where(x > m, jnp.maximum(n[m] - cap2, 0), 0)
    turn = over_at + rank - cap2
    extra8 = to & (rank >= cap2)
    via8, k8 = jnp.zeros(eight, I32), jnp.zeros(eight, I32)
    found8 = jnp.zeros(eight, I32)
    free_at = jnp.zeros(eight, I32)
    for m in range(CHIPS):
        free = jnp.maximum(cap2 - n[m], 0)
        hit = extra8 & (turn >= free_at) & (turn < free_at + free)
        via8 = jnp.where(hit, m, via8)
        k8 = jnp.where(hit, n[m] + turn - free_at, k8)
        found8 = jnp.where(hit, 1, found8)
        free_at += free
    extra = down(extra8, 1)
    found = down(extra8, found8)
    via = jnp.where(extra > 0, down(extra8, via8), x)
    k = jnp.where(extra > 0, down(extra8, k8), down(to, rank))
    moved = (extra > 0) & (sub == via)
    s = down(moved, times(moved.astype(f32), same_half & upper))
    here = zc == z_me

    def prefix(hot):
        hot_f = hot.astype(f32)
        inside, total = times(hot_f, upper), times(hot_f, ll[0] >= 0)
        rows, at = [], jnp.zeros(total.shape[1:], I32)
        for r in range(ROWS_R):
            rows.append((inside[r] + at)[None])
            at = at + total[r]
        return down(hot, jnp.concatenate(rows, axis=0))

    w = prefix(here & (iota((ROWS_R, 16, BLOCK), 1) == via * CHIPS + xd))
    for_chip = (pos // 2) == z_me * CHIPS + x_me
    head = lane % HD
    unit = prefix(for_chip & (sub == cd * HD + head)) + head * BLK_DEV + cd * ITEMS
    key = (zc * CHIPS + via) * CHIPS + xd
    counts = jnp.zeros((BLOCK, BLOCK), f32)
    for r in range(ROWS_R):
        counts += (ll[0] == key[r]).astype(f32)
    full = jnp.max(jnp.sum(counts, axis=1, keepdims=True)) > cap3
    bad = jnp.max(jnp.where((extra > 0) & ((s >= 2 * S1) | (found == 0)), 1, 0)) > 0
    flag_ref[...] = jnp.full((8, BLOCK), jnp.where(full | bad, 1.0, 0.0), f32)
    zslot, rslot, zcore = zc * k2 + k % k2, slab * k2 + k % k2, k // k2
    xout, xin, xcore = xd * k3 + w % k3, via * k3 + w % k3, w // k3
    s_at = (s // S1) * (CHIPS * S1) + s % S1
    in_slab = slab == z_me
    is_extra = extra > 0
    zpool = zcore * (SLABS * k2) + zslot
    mid = here & (via == x_me)
    mine = pos == me
    offsets, total = table_offsets(k2, k3)
    p2, p3 = 2 * SLABS * k2, 2 * CHIPS * k3
    entries = [
        (CHIPS * S1, in_slab & is_extra & (x == x_me) & (s // S1 == c_me), via * S1 + s % S1, q),
        (SLABS * k2, in_slab & (via == x_me) & (zcore == c_me), zslot, jnp.where(is_extra, POOL + s_at + x * S1, q)),
        (CHIPS * k3, mid & (xcore == c_me), xout, jnp.minimum(zcore * (SLABS * k2) + rslot, p2 - 1)),
        (ITEMS, mine, unit - c_me * ITEMS, jnp.minimum(xcore * (CHIPS * k3) + xin, p3 - 1)),
        (CHIPS * k3, for_chip & (xcore == c_me), xin, jnp.minimum(unit, POOL - 1)),
        (SLABS * k2, mid & (zcore == c_me), rslot, jnp.minimum(xcore * (CHIPS * k3) + xout, p3 - 1)),
        (CHIPS * S1, in_slab & is_extra & (via == x_me) & (s // S1 == c_me), x * S1 + s % S1, jnp.minimum(zpool, p2 - 1)),
        (
            ITEMS,
            (row == me // 4) & (lane // ITEMS == me % 4),
            lane % ITEMS,
            jnp.minimum(jnp.where(is_extra, p2 + s_at + via * S1, zpool), p2 + ITEMS - 1),
        ),
        (ITEMS, mine, unit - c_me * ITEMS, ids),
    ]
    parts = []
    for size, mask, slot, value in entries:
        size = -(-size // 8) * 8
        target = jnp.where(mask, slot, -1)
        acc = jnp.zeros((size, BLOCK), I32)
        rows = iota((size, BLOCK), 0)
        for r in range(ROWS_R):
            acc += jnp.where(rows == target[r], value[r], 0)
        parts.append(acc.astype(f32))
    group = jnp.sum(parts.pop(), axis=1, keepdims=True)
    parts.append(jnp.zeros((PAD - total, BLOCK), f32))
    everything = jnp.concatenate(parts, axis=0).astype(bf16)
    tab_ref[...] = mm(jnp.ones((8, BLOCK), bf16), everything, NT).astype(I32)
    for h in range(HD):
        rows = group[h * BLK_DEV : (h + 1) * BLK_DEV]
        for j in range(BLK_DEV):
            one = group[h * BLK_DEV + j : h * BLK_DEV + j + 1]
            tile = jnp.where(jnp.broadcast_to(rows, (BLK_DEV, BLOCK)) == jnp.broadcast_to(one, (BLK_DEV, BLOCK)), 0.0, NEG)
            bias_ref[h, :, j * BLOCK : (j + 1) * BLOCK] = tile


def fast_routing(cluster_ids, caps, me=None, interpret=False):
    slab_of, pos = place_consts()
    vmem = pl.BlockSpec(memory_space=pltpu.VMEM)
    return pl.pallas_call(
        functools.partial(routing_kernel, caps, me),
        out_shape=[
            jax.ShapeDtypeStruct((8, PAD), I32),
            jax.ShapeDtypeStruct((HD, BLK_DEV, TOK), jnp.float32),
            jax.ShapeDtypeStruct((8, BLOCK), jnp.float32),
        ],
        in_specs=[vmem] * 3,
        out_specs=[vmem] * 3,
        scratch_shapes=[pltpu.VMEM((ROWS_R, 1, BLOCK), I32)],
        interpret=interpret,
    )(cluster_ids.reshape(ROWS_R, 1, BLOCK), jnp.asarray(slab_of), jnp.asarray(pos))


FORWARD_SCRATCH = (
    pltpu.VMEM((HD, BLOCK, TOK), jnp.float32),
    pltpu.VMEM((HD, 8, TOK), jnp.float32),
    pltpu.VMEM((TOK, TOK), jnp.float32),
    pltpu.VMEM((TOK, TOK), jnp.bfloat16),
)
BACKWARD_SCRATCH = (pltpu.VMEM((TOK, BLOCK), jnp.float32), pltpu.VMEM((BLOCK, TOK), jnp.float32))
UNITS = jax.ShapeDtypeStruct((ITEMS, BLOCK, BLOCK), jnp.bfloat16)
TOKENS = jax.ShapeDtypeStruct((TOK, WIDTH), jnp.bfloat16)


CHUNKS = 4
SETS = 8
ROWS = 256


class Heads:
    def __init__(self, sems):
        self.y = lax.axis_index("head")
        self.others = [lax.rem(self.y + d, 4) for d in range(1, 4)]
        self.sends, self.recvs = sems

    def copy(self, kind, d, src, dst):
        return pltpu.make_async_remote_copy(
            src_ref=src,
            dst_ref=dst,
            send_sem=self.sends.at[kind, d],
            recv_sem=self.recvs.at[kind, d],
            device_id={"head": self.others[d]},
            device_id_type=MESH,
        )

    def columns(self, y):
        return pl.ds(pl.multiple_of(y * WIDTH, WIDTH), WIDTH)


def layer_kernel(caps, tab, flag, qk, values, cot, weight, bias, output, grad_qk, grad_values, any_flag, *scratch):
    scratch = list(scratch)
    attt, lse, s_ref, p_ref, acc, acct = scratch[:6]
    x_u, v_u, g_u, att_u, gv_u, tokens, parts_in, parts_out, flags = scratch[6:15]
    heads = Heads(scratch[15:17])
    ready = scratch[17]
    gx_u = att_u
    tasks = chunked(6, CHUNKS)
    link = Link(tab, tasks, [True] * 3 + [False] * 3, CHUNKS, *caps, scratch[18:], SETS)
    srcs = (qk, values, tokens, att_u, gx_u, gv_u)
    outs = (x_u, v_u, g_u, tokens, grad_qk, grad_values)
    link.barrier(heads.others)

    def step(stages, *which):
        for i in which:
            for stage in stages:
                if 0 <= i < len(tasks):
                    arr = tasks[i][0]
                    link.run(stage, tasks[i], srcs[arr], outs[arr])

    def each(stage, which):
        for i in which:
            step(stage, i)

    flags[heads.y] = flag[...]
    flag_cps = [heads.copy(0, d, flag, flags.at[heads.y]) for d in range(3)]
    cot_cps = [heads.copy(1, d, cot, parts_in.at[heads.y]) for d in range(3)]

    def tick(t):
        step("H", t - 2)
        step("E", t)
        if t + 2 < 8:
            step("D", t + 2)
        if t + 3 < 8:
            step("C", t + 3)
        if t + 4 < 8:
            step("B", t + 4)
        if t + 5 < 8:
            step("A", t + 5)
        step("F", t)
        step("G", t - 1)

    tick(-5)
    for cp in flag_cps + [cot_cps[1], cot_cps[0], cot_cps[2]]:
        cp.start()
    for t in range(-4, 7):
        tick(t)

    for cp in cot_cps:
        cp.wait()

    @pl.loop(0, TOK // ROWS)
    def _(r):
        at = pl.ds(pl.multiple_of(r * ROWS, ROWS), ROWS)
        total = mm(cot[at, :], weight[:, heads.columns(heads.y)], NT)
        for other in heads.others:
            total += mm(parts_in[other, at, :], weight[:, heads.columns(other)], NT)
        tokens[at, :] = total.astype(jnp.bfloat16)

    for other in heads.others:
        pl.semaphore_signal(ready, inc=1, device_id={"head": other}, device_id_type=MESH)

    each("A", range(8, 12))
    each("B", range(8, 12))
    step("CD", 8)
    step("H", 5)
    step("E", 7)
    step("CD", 9)
    step("F", 7)
    step("G", 6)
    step("CD", 10)
    step("H", 6)
    step("E", 8)
    step("CD", 11)
    step("F", 8)
    step("G", 7)
    step("H", 7)
    step("E", 9)
    step("F", 9)
    step("G", 8)

    @pl.loop(0, HD)
    def _(h):
        head_forward(h, x_u, v_u, bias, att_u, attt, lse, s_ref, p_ref)

    each("A", range(12, 16))
    each("B", range(12, 15))
    step("H", 8)
    step("E", 10)
    step("CD", 12)
    step("F", 10)
    step("G", 9)
    step("B", 15)
    step("CD", 13)
    step("H", 9)
    step("E", 11)
    step("CD", 14)
    step("F", 11)
    step("G", 10)
    step("CD", 15)
    step("H", 10)
    step("E", 12)
    step("G", 11)
    step("F", 12)
    step("H", 11)
    step("E", 13)
    step("F", 13)
    step("G", 12)

    @pl.loop(0, HD)
    def _(h):
        head_backward(h, x_u, v_u, g_u, bias, attt, lse, gx_u, gv_u, acc, acct)

    each("A", range(16, 20))
    step("G", 13)
    each("B", range(16, 20))
    step("H", 12)
    step("E", 14)
    step("CD", 16)
    step("F", 14)
    step("CD", 17)
    step("H", 13)
    step("E", 15)
    step("CD", 18)
    step("F", 15)
    step("G", 14)
    step("CD", 19)
    step("A", 20)
    sums = [heads.copy(2, d, parts_out.at[d], parts_in.at[heads.y]) for d in range(3)]
    for t in range(16, 26):
        step("H", t - 2)
        step("E", t)
        step("D", t + 2 if t >= 18 else -1)
        step("C", t + 3 if t >= 17 else -1)
        step("B", t + 4)
        step("A", t + 5)
        step("F", t)
        step("G", t - 1)
        if t == 17:
            pl.semaphore_wait(ready, 3)
            for d in (1, 0, 2):

                @pl.loop(0, TOK // ROWS)
                def _(r):
                    at = pl.ds(pl.multiple_of(r * ROWS, ROWS), ROWS)
                    part = mm(tokens[at, :], weight[:, heads.columns(heads.others[d])])
                    parts_out[d, at, :] = part.astype(jnp.bfloat16)

                sums[d].start()

            @pl.loop(0, TOK // ROWS)
            def _(r):
                at = pl.ds(pl.multiple_of(r * ROWS, ROWS), ROWS)
                output[at, :] = mm(tokens[at, :], weight[:, heads.columns(heads.y)]).astype(jnp.bfloat16)

    for cp in flag_cps + sums:
        cp.wait()
    any_flag[...] = jnp.max(flags[...], axis=0)

    @pl.loop(0, TOK // ROWS)
    def _(r):
        at = pl.ds(pl.multiple_of(r * ROWS, ROWS), ROWS)
        total = output[at, :].astype(jnp.float32)
        for other in heads.others:
            total += parts_in[other, at, :].astype(jnp.float32)
        output[at, :] = total.astype(jnp.bfloat16)


def layer(tables, flag, qk, values, cot, weight, bias, caps, cid):
    vmem = pl.BlockSpec(memory_space=pltpu.VMEM)
    units = pltpu.VMEM((ITEMS, BLOCK, BLOCK), jnp.bfloat16)
    tokens = pltpu.VMEM((TOK, WIDTH), jnp.bfloat16)
    scratch = list(FORWARD_SCRATCH + BACKWARD_SCRATCH) + [units] * 5 + [tokens]
    scratch += [
        pltpu.VMEM((4, TOK, WIDTH), jnp.bfloat16),
        pltpu.VMEM((3, TOK, WIDTH), jnp.bfloat16),
        pltpu.VMEM((4, 8, BLOCK), jnp.float32),
        pltpu.SemaphoreType.DMA((3, 3)),
        pltpu.SemaphoreType.DMA((3, 3)),
        pltpu.SemaphoreType.REGULAR,
    ]
    return pl.pallas_call(
        functools.partial(layer_kernel, caps),
        out_shape=[TOKENS] * 3 + [jax.ShapeDtypeStruct((8, BLOCK), jnp.float32)],
        in_specs=[pl.BlockSpec(memory_space=pltpu.SMEM)] + [vmem] * 6,
        out_specs=[vmem] * 4,
        scratch_shapes=scratch + link_scratch(SETS, CHUNKS, *caps),
        compiler_params=pltpu.CompilerParams(
            collective_id=cid, has_side_effects=True, vmem_limit_bytes=VMEM_BYTES
        ),
    )(tables, flag, qk, values, cot, weight, bias)


def attention_kernel(x_ref, v_ref, g_ref, bias_ref, att, gx_ref, gv_ref, attt, lse, s_ref, p_ref, acc, acct):
    @pl.loop(0, HD)
    def _(h):
        head_forward(h, x_ref, v_ref, bias_ref, att, attt, lse, s_ref, p_ref)
        head_backward(h, x_ref, v_ref, g_ref, bias_ref, attt, lse, gx_ref, gv_ref, acc, acct)


def attention(x, v, g, bias):
    vmem = pl.BlockSpec(memory_space=pltpu.VMEM)
    return pl.pallas_call(
        attention_kernel,
        out_shape=[UNITS] * 3,
        in_specs=[vmem] * 4,
        out_specs=[vmem] * 3,
        scratch_shapes=list(FORWARD_SCRATCH + BACKWARD_SCRATCH),
        compiler_params=pltpu.CompilerParams(vmem_limit_bytes=VMEM_BYTES),
    )(x, v, g, bias)


def model_output(attended, out_weight):
    partial_term = jnp.dot(attended, out_weight, preferred_element_type=jnp.float32)
    return lax.psum_scatter(partial_term.astype(jnp.bfloat16), "head", scatter_dimension=1, tiled=True)


def cotangent_heads(out_cotangent, out_weight):
    gathered = lax.all_gather(out_cotangent, "head", axis=1, tiled=True)
    return jnp.einsum("tn,kn->tk", gathered, out_weight, preferred_element_type=jnp.float32).astype(
        jnp.bfloat16
    )


def per_device(qk, values, out_weight, out_cotangent, cluster_ids):
    tables, bias, flag = fast_routing(cluster_ids, FAST)
    *fast, any_lost = layer(tables, flag, qk, values, out_cotangent, out_weight, bias, FAST, 0)

    def slow(args):
        me = lax.axis_index("seq").astype(I32)
        place = choose_places((cluster_ids // CL_OWN).reshape(N_SEQ, ITEMS))
        tables, bias, _ = routing(me, cluster_ids, place, *FULL)
        tables = tables[None]
        grad_attended = cotangent_heads(out_cotangent, out_weight)
        sources = jnp.stack([qk, values, grad_attended])
        x, v, g = lax.map(lambda a: exchange(tables, a, True, FULL, 1), sources)
        units = jnp.stack(attention(x, v, g, bias))
        home = lax.map(lambda a: exchange(tables, a, False, FULL, 2), units)
        return [model_output(home[0], out_weight), home[1], home[2]]

    return tuple(lax.cond(any_lost[0, 0] > 0, slow, lambda args: args, fast))


def solution(mesh):
    return jax.shard_map(
        per_device,
        mesh=mesh,
        in_specs=(
            P("seq", "head"),
            P("seq", "head"),
            P("head", None),
            P("seq", "head"),
            P(None, "head"),
        ),
        out_specs=(P("seq", "head"), P("seq", "head"), P("seq", "head")),
        check_vma=False,
    )
```

```python
import functools
import math

import jax
import jax.numpy as jnp
import numpy as np
from jax import lax
from jax.experimental import pallas as pl
from jax.experimental.pallas import tpu as pltpu
from jax.sharding import PartitionSpec as P

BLOCK = 128
CL_OWN = 2
N_SEQ = 64
SLABS = 8
CHIPS = 4
ITEMS = 32
POOL = 2 * ITEMS
HD = 4
BLK_DEV = 8
NBLK = 512
TOK = 1024
WIDTH = 512
S1 = 4
I32 = jnp.int32
MESH = pl.DeviceIdType.MESH
NEG = -1e30
LOG2E = math.log2(math.e)
FAST = (5, 15)
FULL = (16, 32)
VMEM_BYTES = 60 * 1024 * 1024


def rng_(n): return jnp.arange(n,dtype=I32)
def pick(hit,value): return jnp.sum(jnp.where(hit,value,0),axis=-1).astype(I32)
def places():
    owner=np.arange(N_SEQ); maps=[]
    for width,mults in ((1,(1,)),(2,(1,3,5,7)),(4,range(1,16,2)),(8,range(1,32,2))):
        for mult in mults:
            e=(mult*owner)%N_SEQ
            maps.append((e//width)%SLABS*8+(e//(width*SLABS))*width+e%width)
    r=np.random.RandomState(7)
    while len(maps)<32: maps.append(r.permutation(N_SEQ))
    return np.stack(maps).astype(np.int32)
PLACES=places()
def choose_places(owners):
    cnt=jnp.sum((owners[:,:,None]==rng_(N_SEQ)).astype(I32),axis=1)
    slab_cnt=jnp.sum(cnt.reshape(SLABS,8,N_SEQ),axis=1)
    n=PLACES.shape[0]
    slab_of=np.zeros((N_SEQ,n*SLABS),np.float32)
    for p in range(n): slab_of[np.arange(N_SEQ),p*SLABS+PLACES[p]//8]=1
    loads=jnp.dot(slab_cnt.astype(jnp.float32),jnp.asarray(slab_of),preferred_element_type=jnp.float32,precision="highest")
    worst=jnp.max(loads.reshape(SLABS,n,SLABS),axis=(0,2))
    best=jnp.argmin(worst).astype(I32)
    return jnp.sum(jnp.where((rng_(n)==best)[:,None],PLACES,0),axis=0)
def routing(me,cluster_ids,place,k2,k3):
    owners=(cluster_ids//CL_OWN).reshape(-1)
    z_me,x_me,c_me=me//8,(me//2)%4,me%2
    cap2,cap3=2*k2,2*k3
    pos=jnp.sum(jnp.where(owners[:,None]==rng_(N_SEQ),place,0),axis=1)
    zc=(pos//8).reshape(SLABS,CHIPS,POOL)
    earlier=rng_(POOL)[None,:]<rng_(POOL)[:,None]
    r=jnp.sum(((zc[...,:,None]==zc[...,None,:])&earlier).astype(I32),axis=-1)
    to=zc[...,None]==rng_(SLABS)
    n=jnp.sum(to.astype(I32),axis=2)
    over,free=jnp.maximum(n-cap2,0),jnp.maximum(cap2-n,0)
    below=(rng_(CHIPS)[None,:]<rng_(CHIPS)[:,None]).astype(I32)
    over_at=jnp.sum(below[None,:,:,None]*over[:,None],axis=2)
    free_at=jnp.sum(below[None,:,:,None]*free[:,None],axis=2)
    extra=r>=cap2
    turn=jnp.sum(jnp.where(to,over_at[:,:,None,:],0),axis=-1)+r-cap2
    def at(v):
        return jnp.sum(jnp.where(to[:,:,:,None,:],v[:,None,None,:,:],0),axis=-1)
    f0=at(free_at)
    hit=extra[...,None]&(f0<=turn[...,None])&(turn[...,None]<f0+at(free))
    own_chip=rng_(CHIPS)[None,:,None]
    via=jnp.where(extra,pick(hit,rng_(CHIPS)),own_chip)
    k=jnp.where(extra,pick(hit,at(n)+turn[...,None]-f0),r)
    s=jnp.sum((extra[...,None,:]&(via[...,:,None]==via[...,None,:])&earlier).astype(I32),axis=-1)
    lost=jnp.any(extra&((s>=2*S1)|~jnp.any(hit,-1)))
    slab_items=CHIPS*POOL
    zf,via,k,s,extra=[v.reshape(SLABS,slab_items) for v in (zc,via,k,s,extra)]
    src=jnp.broadcast_to(own_chip,(SLABS,CHIPS,POOL)).reshape(SLABS,slab_items)
    pos=pos.reshape(SLABS,slab_items)
    xd=(pos//2)%4
    here=zf==z_me
    key=jnp.where(here,via*4+xd,-1)
    before=rng_(slab_items)[None,:]<rng_(slab_items)[:,None]
    w=jnp.sum(((key[:,:,None]==key[:,None,:])&before).astype(I32),axis=-1)
    keyed=key[...,None]==rng_(16)
    hist=jnp.sum(keyed.astype(I32),axis=1)
    upto=(rng_(SLABS)[None,:]<rng_(SLABS)[:,None]).astype(I32)
    base=jnp.sum(upto[:,:,None]*hist[None],axis=1)
    w=w+jnp.sum(jnp.where(keyed,base[:,None,:],0),axis=-1)
    full_key=(zf*CHIPS+via)*CHIPS+xd
    counts=jnp.sum((full_key.reshape(-1,1)==rng_(SLABS*CHIPS*CHIPS)).astype(I32),axis=0)
    lost=lost|(jnp.max(counts)>cap3)
    zslot=zf*k2+k%k2
    rslot=rng_(SLABS)[:,None]*k2+k%k2
    zcore=k//k2
    xslot_out=xd*k3+w%k3
    xslot_in=via*k3+w%k3
    xcore=w//k3
    s_at=(s//S1)*(CHIPS*S1)+s%S1
    row=lambda v: lax.dynamic_index_in_dim(v,z_me,0,keepdims=False)
    R=lambda m: rng_(m)[:,None]
    zf_r,via_r,k_r,s_r,ex_r,src_r,zslot_r,zcore_r,sat_r=[row(v) for v in (zf,via,k,s,extra,src,zslot,zcore,s_at)]
    q=rng_(slab_items)%POOL
    t1=pick(ex_r&(src_r==x_me)&(s_r//S1==c_me)&(via_r*S1+s_r%S1==R(CHIPS*S1)),q)
    t2=pick((via_r==x_me)&(zcore_r==c_me)&(zslot_r==R(SLABS*k2)),jnp.where(ex_r,POOL+sat_r+src_r*S1,q))
    r1=pick(ex_r&(via_r==x_me)&(s_r//S1==c_me)&(src_r*S1+s_r%S1==R(CHIPS*S1)),zcore_r*(SLABS*k2)+zslot_r)
    back=jnp.where(ex_r,2*SLABS*k2+sat_r+via_r*S1,zcore_r*(SLABS*k2)+zslot_r)
    rf=lax.dynamic_slice_in_dim(back,x_me*POOL+c_me*ITEMS,ITEMS,0)
    mid=here&(via==x_me)
    fl=lambda v: v.reshape(-1)
    t3=pick(fl(mid&(xcore==c_me))&(fl(xslot_out)==R(CHIPS*k3)),fl(zcore*(SLABS*k2)+rslot))
    r2=pick((mid&(zcore==c_me))[:,None,:]&((k%k2)[:,None,:]==rng_(k2)[None,:,None]),(xcore*(CHIPS*k3)+xslot_out)[:,None,:]).reshape(-1)
    chip_me=z_me*4+x_me
    heads=lambda v: v.reshape(NBLK,HD).T
    pos_h=heads(pos)
    both=jnp.stack([pos_h==chip_me*2,pos_h==chip_me*2+1])
    upper=jnp.asarray(np.triu(np.ones((NBLK,NBLK)),1),jnp.bfloat16)
    rank=jnp.dot(both.reshape(2*HD,NBLK).astype(jnp.bfloat16),upper,preferred_element_type=jnp.float32).astype(I32).reshape(2,HD,NBLK)
    unit=rank+BLK_DEV*rng_(HD)[None,:,None]+ITEMS*rng_(2)[:,None,None]
    unit=jnp.sum(jnp.where(both,unit,0),axis=0)
    for_chip=both[0]|both[1]
    xin_h,xcore_h=heads(xslot_in),heads(xcore)
    r3=pick((for_chip&(xcore_h==c_me)).reshape(-1)&(xin_h.reshape(-1)==R(CHIPS*k3)),unit.reshape(-1))
    mine=pos_h==me
    slot=mine[:,None,:]&((unit-c_me*ITEMS)[:,None,:]==(rng_(HD)*BLK_DEV)[:,None,None]+rng_(BLK_DEV)[None,:,None])
    tu=pick(slot,(xcore_h*(CHIPS*k3)+xin_h)[:,None,:]).reshape(-1)
    group=pick(slot,cluster_ids.T[:,None,:])
    pad=lambda v,m: jnp.clip(v,0,m)
    P2,P3=2*SLABS*k2,2*CHIPS*k3
    tables=jnp.concatenate([t1,t2,pad(t3,P2-1),pad(tu,P3-1),pad(r3,POOL-1),pad(r2,P3-1),pad(r1,P2-1),pad(rf,P2+2*CHIPS*S1-1)])
    same=group[:,:,None]==group[:,None,:]
    bias=jnp.where(jnp.repeat(same,BLOCK,axis=2),0.0,NEG).astype(jnp.float32)
    return tables,bias,lost


class Link:
    def __init__(self, tab, tasks, inbound, chunks, k2, k3, scratch, sets):
        self.tab, self.k2, self.k3, self.rows = tab, k2, k3, BLOCK // chunks
        self.tasks, self.inbound = tasks, inbound
        self.buf = {t: scratch[7 * (i % sets) : 7 * (i % sets) + 7] for i, t in enumerate(tasks)}
        self.sends, self.recvs = scratch[7 * sets : 7 * sets + 2]
        self.index = {t: i % sets for i, t in enumerate(tasks)}
        self.me = lax.axis_index("seq")
        self.z, self.x, self.c = self.me // 8, (self.me // 2) % CHIPS, self.me % 2
        self.t1, self.t2, self.t3, self.tu, self.r3, self.r2, self.r1, self.rf = table_offsets(k2, k3)[0]
        self.live = {}

    def peer(self, axis, d):
        if axis == "z":
            to = lax.rem(self.z + d, SLABS)
            return to, to * 8 + self.x * 2 + self.c
        if axis == "x":
            to = lax.rem(self.x + d, CHIPS)
            return to, self.z * 8 + to * 2 + self.c
        return 1 - self.c, self.me + 1 - 2 * self.c

    def peers(self):
        out = [self.peer("z", d)[1] for d in range(1, SLABS)]
        out += [self.peer("x", d)[1] for d in range(1, CHIPS)]
        return out + [self.peer("c", 1)[1]]

    def barrier(self, extra=()):
        barrier = pltpu.get_barrier_semaphore()
        peers = self.peers()
        for p in peers:
            pl.semaphore_signal(barrier, inc=1, device_id={"seq": p}, device_id_type=MESH)
        for p in extra:
            pl.semaphore_signal(barrier, inc=1, device_id={"head": p}, device_id_type=MESH)
        pl.semaphore_wait(barrier, len(peers) + len(extra))

    def start(self, task, kind, d, src, dst, peer):
        s = self.index[task] * 7 + kind
        cp = pltpu.make_async_remote_copy(
            src_ref=src,
            dst_ref=dst,
            send_sem=self.sends.at[s, d],
            recv_sem=self.recvs.at[s, d],
            device_id={"seq": peer},
            device_id_type=MESH,
        )
        cp.start()
        self.live.setdefault((task, kind), []).append(cp)

    def share(self, task, kind, ref, half):
        part = ref.at[pl.ds(self.c * half, half)]
        self.start(task, kind, 0, part, part, self.peer("c", 1)[1])

    def wait(self, task, kind):
        for cp in self.live[task, kind]:
            cp.wait_recv()

    def sent(self, task, *kinds):
        for kind in kinds:
            for cp in self.live.pop((task, kind)):
                cp.wait_send()

    def pack(self, task, kind, axis, load, send, recv, count, base):
        n = SLABS if axis == "z" else CHIPS
        order = (4, 3, 5, 2, 6, 1, 7, 0) if axis == "z" else (2, 1, 3, 0)
        mine = self.z if axis == "z" else self.x
        at = self.c * (n * count) + mine * count
        for d in order:
            to, peer = self.peer(axis, d)

            @pl.loop(0, count, unroll=True)
            def _(k):
                tile = load(self.tab[0, base + to * count + k])
                if d == 0:
                    recv[at + k] = tile
                else:
                    send[to * count + k] = tile

            if d:
                self.start(task, kind, d, send.at[pl.ds(to * count, count)], recv.at[pl.ds(at, count)], peer)

    def either(self, first, second, size):
        def load(i):
            a = first[jnp.minimum(i, size - 1)]
            b = second[jnp.maximum(i - size, 0)]
            return jnp.where(i < size, a, b)

        return load

    def run(self, stage, task, src=None, out=None):
        pool, s1, arr, zs, zr, xs, xr = self.buf[task]
        k2, k3, rows = self.k2, self.k3, self.rows
        c = task[1]
        at = slice(c * rows, (c + 1) * rows)
        inward = self.inbound[task[0]]
        if stage == "A":
            if inward:
                for j in range(ITEMS):
                    b, h = j // HD, j % HD
                    pool[self.c * ITEMS + j] = src[
                        b * BLOCK + c * rows : b * BLOCK + (c + 1) * rows, h * BLOCK : (h + 1) * BLOCK
                    ]
            else:

                @pl.loop(0, ITEMS, unroll=8)
                def _(u):
                    pool[self.c * ITEMS + u] = src[u, at, :]

            self.share(task, 0, pool, ITEMS)
        elif stage == "B":
            self.wait(task, 0)
            if inward:
                self.pack(task, 1, "x", lambda i: pool[i], s1, arr, S1, self.t1)
            else:
                self.pack(task, 5, "x", lambda i: pool[i], xs, xr, k3, self.r3)
        elif stage == "C":
            if inward:
                self.wait(task, 1)
                self.share(task, 2, arr, CHIPS * S1)
            else:
                self.wait(task, 5)
                self.share(task, 6, xr, CHIPS * k3)
        elif stage == "D":
            if inward:
                self.wait(task, 2)
                self.sent(task, 0, 1, 2)
                self.pack(task, 3, "z", self.either(pool, arr, POOL), zs, zr, k2, self.t2)
            else:
                self.wait(task, 6)
                self.sent(task, 0, 5, 6)
                self.pack(task, 3, "z", lambda i: xr[i], zs, zr, k2, self.r2)
        elif stage == "E":
            self.wait(task, 3)
            self.share(task, 4, zr, SLABS * k2)
        elif stage == "F":
            self.wait(task, 4)
            self.sent(task, 3, 4)
            if inward:
                self.pack(task, 5, "x", lambda i: zr[i], xs, xr, k3, self.t3)
            else:
                self.pack(task, 1, "x", lambda i: zr[i], s1, arr, S1, self.r1)
        elif stage == "G":
            if inward:
                self.wait(task, 5)
                self.share(task, 6, xr, CHIPS * k3)
            else:
                self.wait(task, 1)
                self.share(task, 2, arr, CHIPS * S1)
        elif stage == "H":
            if inward:
                self.wait(task, 6)
                self.sent(task, 5, 6)

                @pl.loop(0, ITEMS, unroll=8)
                def _(u):
                    out[u, at, :] = xr[self.tab[0, self.tu + u]]
            else:
                self.wait(task, 2)
                self.sent(task, 1, 2)
                load = self.either(zr, arr, 2 * SLABS * k2)

                @pl.loop(0, BLK_DEV)
                def _(b):
                    for h in range(HD):
                        out[pl.ds(pl.multiple_of(b * BLOCK + c * rows, rows), rows), h * BLOCK : (h + 1) * BLOCK] = load(
                            self.tab[0, self.rf + b * HD + h]
                        )


def link_scratch(sets, chunks, k2, k3):
    sizes = (POOL, CHIPS * S1, ITEMS, SLABS * k2, 2 * SLABS * k2, CHIPS * k3, 2 * CHIPS * k3)
    out = []
    for _ in range(sets):
        out += [pltpu.VMEM((s, BLOCK // chunks, BLOCK), jnp.bfloat16) for s in sizes]
    return out + [pltpu.SemaphoreType.DMA((7 * sets, 8))] * 2


def chunked(arrays, chunks):
    return tuple((arr, c) for arr in range(arrays) for c in range(chunks))


def exchange_kernel(inward, caps, tab, src, out, *scratch):
    task = (0, 0)
    link = Link(tab, [task], [inward], 1, *caps, scratch, 1)
    link.barrier()
    for stage in "ABCDEFGH":
        link.run(stage, task, src, out)


def exchange(tables, array, inward, caps, cid):
    vmem = pl.BlockSpec(memory_space=pltpu.VMEM)
    return pl.pallas_call(
        functools.partial(exchange_kernel, inward, caps),
        out_shape=UNITS if inward else TOKENS,
        in_specs=[pl.BlockSpec(memory_space=pltpu.SMEM), vmem],
        out_specs=vmem,
        scratch_shapes=link_scratch(1, 1, *caps),
        compiler_params=pltpu.CompilerParams(
            collective_id=cid, has_side_effects=True, vmem_limit_bytes=VMEM_BYTES
        ),
    )(tables, array)


NT = (((1,), (1,)), ((), ()))
TN = (((0,), (0,)), ((), ()))


def mm(a, b, dims=(((1,), (0,)), ((), ()))):
    return lax.dot_general(a, b, dims, preferred_element_type=jnp.float32)


def diagonal():
    shape = (BLOCK, BLOCK)
    return lax.broadcasted_iota(I32, shape, 0) == lax.broadcasted_iota(I32, shape, 1)


def of_head(ref, h):
    return ref[pl.ds(h * BLK_DEV, BLK_DEV)].reshape(TOK, BLOCK)


def head_forward(h, x_ref, v_ref, bias_ref, att_ref, attt_ref, lse_ref, s_ref, p_ref):
    c2 = (BLOCK ** -0.5) * LOG2E
    x = of_head(x_ref, h)
    diag = diagonal()
    m = jnp.full((1, TOK), NEG, jnp.float32)
    for i in range(BLK_DEV):
        at = slice(i * BLOCK, (i + 1) * BLOCK)
        s_ref[at, :] = mm(x[at, :], x, NT)
        s_ref[at, at] = jnp.where(diag, NEG, s_ref[at, at])
        top = jnp.max(s_ref[at, :], axis=0, keepdims=True)
        m = jnp.maximum(m, top * c2 + bias_ref[h, i : i + 1, :])
    l = jnp.zeros((1, TOK), jnp.float32)
    for i in range(BLK_DEV):
        at = slice(i * BLOCK, (i + 1) * BLOCK)
        p = jnp.exp2(s_ref[at, :] * c2 + (bias_ref[h, i : i + 1, :] - m))
        l = l + jnp.sum(p, axis=0, keepdims=True)
        p_ref[at, :] = p.astype(jnp.bfloat16)
    attt = mm(of_head(v_ref, h), p_ref[...], TN) * (1.0 / l)
    attt_ref[h] = attt
    att_ref[pl.ds(h * BLK_DEV, BLK_DEV)] = attt.T.astype(jnp.bfloat16).reshape(BLK_DEV, BLOCK, BLOCK)
    lse_ref[h] = jnp.broadcast_to(m + jnp.log2(l), (8, TOK))


def head_backward(h, x_ref, v_ref, g_ref, bias_ref, attt_ref, lse_ref, gx_ref, gv_ref, acc_ref, acct_ref):
    c2 = (BLOCK ** -0.5) * LOG2E
    x = of_head(x_ref, h)
    g = of_head(g_ref, h)
    diag = diagonal()
    delta = jnp.sum(g.astype(jnp.float32).T * attt_ref[h], axis=0, keepdims=True)
    lse = lse_ref[h, 0:1, :]
    for i in range(BLK_DEV):
        at = slice(i * BLOCK, (i + 1) * BLOCK)
        x_i = x[at, :]
        p = jnp.exp2(mm(x_i, x, NT) * c2 + (bias_ref[h, i : i + 1, :] - lse))
        own = jnp.where(diag, 0.0, p[:, at])
        parts = [p[:, : i * BLOCK]] * (i > 0) + [own] + [p[:, (i + 1) * BLOCK :]] * (i < BLK_DEV - 1)
        p = jnp.concatenate(parts, axis=1)
        gs = p * (mm(v_ref[h * BLK_DEV + i], g, NT) - delta)
        gv_ref[h * BLK_DEV + i] = mm(p.astype(jnp.bfloat16), g).astype(jnp.bfloat16)
        gsb = gs.astype(jnp.bfloat16)
        acc_ref[at, :] = mm(gsb, x)
        add = mm(x_i, gsb, TN)
        if i == 0:
            acct_ref[...] = add
        else:
            acct_ref[...] += add
    gx = (acc_ref[...] + acct_ref[...].T) * (BLOCK ** -0.5)
    gx_ref[pl.ds(h * BLK_DEV, BLK_DEV)] = gx.astype(jnp.bfloat16).reshape(BLK_DEV, BLOCK, BLOCK)


ROWS_R = 16
PAD = 512


def place_consts():
    n = PLACES.shape[0]
    slab_of = np.zeros((n * SLABS, N_SEQ), np.float32)
    for p in range(n):
        slab_of[p * SLABS + PLACES[p] // 8, np.arange(N_SEQ)] = 1
    pos = np.zeros((N_SEQ, BLOCK), np.float32)
    pos[:, :n] = PLACES.T
    return slab_of, pos


def table_offsets(k2, k3):
    at, out = 0, []
    for size in (CHIPS * S1, SLABS * k2, CHIPS * k3, ITEMS, CHIPS * k3, SLABS * k2, CHIPS * S1, ITEMS):
        out.append(at)
        at += -(-size // 8) * 8
    return out, at


def routing_kernel(caps, me, ids_ref, slab_of_ref, places_ref, tab_ref, bias_ref, flag_ref, pos_ref):
    k2, k3 = caps
    cap2, cap3 = 2 * k2, 2 * k3
    f32, bf16 = jnp.float32, jnp.bfloat16
    if me is None:
        me = lax.axis_index("seq")
    z_me, x_me, c_me = me // 8, (me // 2) % CHIPS, me % 2
    iota = lambda shape, axis: lax.broadcasted_iota(I32, shape, axis)
    item = (ROWS_R, 1, BLOCK)
    row, lane = iota(item, 0), iota(item, 2)
    ids = ids_ref[...]
    owner = ids // CL_OWN
    own_iota = iota((N_SEQ, BLOCK), 0)
    ll = (iota((BLOCK, BLOCK), 0), iota((BLOCK, BLOCK), 1))
    cnt = jnp.zeros((N_SEQ, BLOCK), f32)
    for z in range(SLABS):
        both = (own_iota == owner[2 * z]).astype(f32) + (own_iota == owner[2 * z + 1]).astype(f32)
        cnt += mm(both.astype(bf16), (ll[1] == z).astype(f32).astype(bf16))
    loads = mm(slab_of_ref[...].astype(bf16), cnt.astype(bf16))
    n_place = slab_of_ref.shape[0] // SLABS
    worst = jnp.max(jnp.max(loads.reshape(n_place, SLABS, BLOCK), axis=1), axis=1, keepdims=True)
    best = jnp.min(worst.astype(I32) * 64 + iota((n_place, 1), 0)) % 64
    chosen = jnp.where(iota((N_SEQ, BLOCK), 1) == best, places_ref[...], 0.0)
    place = jnp.sum(chosen, axis=1, keepdims=True)
    for r in range(ROWS_R):
        pos_ref[r] = jnp.sum(jnp.where(own_iota == owner[r], place, 0.0), axis=0, keepdims=True).astype(I32)
    pos = pos_ref[...]
    zc, xd, cd = pos // 8, (pos // 2) % CHIPS, pos % 2
    half = lane // POOL
    x = (row % 2) * 2 + half
    slab = row // 2
    q = lane % POOL
    same_half = (ll[0] // POOL) == (ll[1] // POOL)
    upper = ll[0] < ll[1]
    as_bf = lambda m: m.astype(f32).astype(bf16)

    def times(hot, matrix):
        n = hot.shape[1]
        return mm(hot.reshape(ROWS_R * n, BLOCK).astype(bf16), as_bf(matrix)).astype(I32).reshape(ROWS_R, n, BLOCK)

    def down(hot, value):
        return jnp.sum(jnp.where(hot, value, 0), axis=1, keepdims=True)

    eight = (ROWS_R, 8, BLOCK)
    sub = iota(eight, 1)
    to = sub == zc
    to_f = to.astype(f32)
    rank = times(to_f, same_half & upper)
    first, second = times(to_f, ll[0] < POOL), times(to_f, ll[0] >= POOL)

    def of_slab(v, which):
        v = v.reshape(SLABS, 2, 8, BLOCK)[:, which : which + 1]
        return jnp.concatenate([v, v], axis=1).reshape(eight)

    n = [of_slab(first, 0), of_slab(second, 0), of_slab(first, 1), of_slab(second, 1)]
    over_at = jnp.zeros(eight, I32)
    for m in range(CHIPS):
        over_at += jnp.where(x > m, jnp.maximum(n[m] - cap2, 0), 0)
    turn = over_at + rank - cap2
    extra8 = to & (rank >= cap2)
    via8, k8 = jnp.zeros(eight, I32), jnp.zeros(eight, I32)
    found8 = jnp.zeros(eight, I32)
    free_at = jnp.zeros(eight, I32)
    for m in range(CHIPS):
        free = jnp.maximum(cap2 - n[m], 0)
        hit = extra8 & (turn >= free_at) & (turn < free_at + free)
        via8 = jnp.where(hit, m, via8)
        k8 = jnp.where(hit, n[m] + turn - free_at, k8)
        found8 = jnp.where(hit, 1, found8)
        free_at += free
    extra = down(extra8, 1)
    found = down(extra8, found8)
    via = jnp.where(extra > 0, down(extra8, via8), x)
    k = jnp.where(extra > 0, down(extra8, k8), down(to, rank))
    moved = (extra > 0) & (sub == via)
    s = down(moved, times(moved.astype(f32), same_half & upper))
    here = zc == z_me

    def prefix(hot):
        hot_f = hot.astype(f32)
        inside, total = times(hot_f, upper), times(hot_f, ll[0] >= 0)
        rows, at = [], jnp.zeros(total.shape[1:], I32)
        for r in range(ROWS_R):
            rows.append((inside[r] + at)[None])
            at = at + total[r]
        return down(hot, jnp.concatenate(rows, axis=0))

    w = prefix(here & (iota((ROWS_R, 16, BLOCK), 1) == via * CHIPS + xd))
    for_chip = (pos // 2) == z_me * CHIPS + x_me
    head = lane % HD
    unit = prefix(for_chip & (sub == cd * HD + head)) + head * BLK_DEV + cd * ITEMS
    key = (zc * CHIPS + via) * CHIPS + xd
    counts = jnp.zeros((BLOCK, BLOCK), f32)
    for r in range(ROWS_R):
        counts += (ll[0] == key[r]).astype(f32)
    full = jnp.max(jnp.sum(counts, axis=1, keepdims=True)) > cap3
    bad = jnp.max(jnp.where((extra > 0) & ((s >= 2 * S1) | (found == 0)), 1, 0)) > 0
    flag_ref[...] = jnp.full((8, BLOCK), jnp.where(full | bad, 1.0, 0.0), f32)
    zslot, rslot, zcore = zc * k2 + k % k2, slab * k2 + k % k2, k // k2
    xout, xin, xcore = xd * k3 + w % k3, via * k3 + w % k3, w // k3
    s_at = (s // S1) * (CHIPS * S1) + s % S1
    in_slab = slab == z_me
    is_extra = extra > 0
    zpool = zcore * (SLABS * k2) + zslot
    mid = here & (via == x_me)
    mine = pos == me
    offsets, total = table_offsets(k2, k3)
    p2, p3 = 2 * SLABS * k2, 2 * CHIPS * k3
    entries = [
        (CHIPS * S1, in_slab & is_extra & (x == x_me) & (s // S1 == c_me), via * S1 + s % S1, q),
        (SLABS * k2, in_slab & (via == x_me) & (zcore == c_me), zslot, jnp.where(is_extra, POOL + s_at + x * S1, q)),
        (CHIPS * k3, mid & (xcore == c_me), xout, jnp.minimum(zcore * (SLABS * k2) + rslot, p2 - 1)),
        (ITEMS, mine, unit - c_me * ITEMS, jnp.minimum(xcore * (CHIPS * k3) + xin, p3 - 1)),
        (CHIPS * k3, for_chip & (xcore == c_me), xin, jnp.minimum(unit, POOL - 1)),
        (SLABS * k2, mid & (zcore == c_me), rslot, jnp.minimum(xcore * (CHIPS * k3) + xout, p3 - 1)),
        (CHIPS * S1, in_slab & is_extra & (via == x_me) & (s // S1 == c_me), x * S1 + s % S1, jnp.minimum(zpool, p2 - 1)),
        (
            ITEMS,
            (row == me // 4) & (lane // ITEMS == me % 4),
            lane % ITEMS,
            jnp.minimum(jnp.where(is_extra, p2 + s_at + via * S1, zpool), p2 + ITEMS - 1),
        ),
        (ITEMS, mine, unit - c_me * ITEMS, ids),
    ]
    parts = []
    for size, mask, slot, value in entries:
        size = -(-size // 8) * 8
        target = jnp.where(mask, slot, -1)
        acc = jnp.zeros((size, BLOCK), I32)
        rows = iota((size, BLOCK), 0)
        for r in range(ROWS_R):
            acc += jnp.where(rows == target[r], value[r], 0)
        parts.append(acc.astype(f32))
    group = jnp.sum(parts.pop(), axis=1, keepdims=True)
    parts.append(jnp.zeros((PAD - total, BLOCK), f32))
    everything = jnp.concatenate(parts, axis=0).astype(bf16)
    tab_ref[...] = mm(jnp.ones((8, BLOCK), bf16), everything, NT).astype(I32)
    for h in range(HD):
        rows = group[h * BLK_DEV : (h + 1) * BLK_DEV]
        for j in range(BLK_DEV):
            one = group[h * BLK_DEV + j : h * BLK_DEV + j + 1]
            tile = jnp.where(jnp.broadcast_to(rows, (BLK_DEV, BLOCK)) == jnp.broadcast_to(one, (BLK_DEV, BLOCK)), 0.0, NEG)
            bias_ref[h, :, j * BLOCK : (j + 1) * BLOCK] = tile


def fast_routing(cluster_ids, caps, me=None, interpret=False):
    slab_of, pos = place_consts()
    vmem = pl.BlockSpec(memory_space=pltpu.VMEM)
    return pl.pallas_call(
        functools.partial(routing_kernel, caps, me),
        out_shape=[
            jax.ShapeDtypeStruct((8, PAD), I32),
            jax.ShapeDtypeStruct((HD, BLK_DEV, TOK), jnp.float32),
            jax.ShapeDtypeStruct((8, BLOCK), jnp.float32),
        ],
        in_specs=[vmem] * 3,
        out_specs=[vmem] * 3,
        scratch_shapes=[pltpu.VMEM((ROWS_R, 1, BLOCK), I32)],
        interpret=interpret,
    )(cluster_ids.reshape(ROWS_R, 1, BLOCK), jnp.asarray(slab_of), jnp.asarray(pos))


FORWARD_SCRATCH = (
    pltpu.VMEM((HD, BLOCK, TOK), jnp.float32),
    pltpu.VMEM((HD, 8, TOK), jnp.float32),
    pltpu.VMEM((TOK, TOK), jnp.float32),
    pltpu.VMEM((TOK, TOK), jnp.bfloat16),
)
BACKWARD_SCRATCH = (pltpu.VMEM((TOK, BLOCK), jnp.float32), pltpu.VMEM((BLOCK, TOK), jnp.float32))
UNITS = jax.ShapeDtypeStruct((ITEMS, BLOCK, BLOCK), jnp.bfloat16)
TOKENS = jax.ShapeDtypeStruct((TOK, WIDTH), jnp.bfloat16)


CHUNKS = 4
SETS = 8
ROWS = 256


class Heads:
    def __init__(self, sems):
        self.y = lax.axis_index("head")
        self.others = [lax.rem(self.y + d, 4) for d in range(1, 4)]
        self.sends, self.recvs = sems

    def copy(self, kind, d, src, dst):
        return pltpu.make_async_remote_copy(
            src_ref=src,
            dst_ref=dst,
            send_sem=self.sends.at[kind, d],
            recv_sem=self.recvs.at[kind, d],
            device_id={"head": self.others[d]},
            device_id_type=MESH,
        )

    def columns(self, y):
        return pl.ds(pl.multiple_of(y * WIDTH, WIDTH), WIDTH)


def layer_kernel(caps, tab, flag, qk, values, cot, weight, bias, output, grad_qk, grad_values, any_flag, *scratch):
    scratch = list(scratch)
    attt, lse, s_ref, p_ref, acc, acct = scratch[:6]
    x_u, v_u, g_u, att_u, gv_u, tokens, parts_in, parts_out, flags = scratch[6:15]
    heads = Heads(scratch[15:17])
    ready = scratch[17]
    gx_u = att_u
    tasks = chunked(6, CHUNKS)
    link = Link(tab, tasks, [True] * 3 + [False] * 3, CHUNKS, *caps, scratch[18:], SETS)
    srcs = (qk, values, tokens, att_u, gx_u, gv_u)
    outs = (x_u, v_u, g_u, tokens, grad_qk, grad_values)
    link.barrier(heads.others)

    def step(stages, *which):
        for i in which:
            for stage in stages:
                if 0 <= i < len(tasks):
                    arr = tasks[i][0]
                    link.run(stage, tasks[i], srcs[arr], outs[arr])

    def each(stage, which):
        for i in which:
            step(stage, i)

    flags[heads.y] = flag[...]
    flag_cps = [heads.copy(0, d, flag, flags.at[heads.y]) for d in range(3)]
    cot_cps = [heads.copy(1, d, cot, parts_in.at[heads.y]) for d in range(3)]

    def tick(t):
        step("H", t - 2)
        step("E", t)
        if t + 2 < 8:
            step("D", t + 2)
        if t + 3 < 8:
            step("C", t + 3)
        if t + 4 < 8:
            step("B", t + 4)
        if t + 5 < 8:
            step("A", t + 5)
        step("F", t)
        step("G", t - 1)

    tick(-5)
    for cp in flag_cps + [cot_cps[1], cot_cps[0], cot_cps[2]]:
        cp.start()
    for t in range(-4, 7):
        tick(t)

    for cp in cot_cps:
        cp.wait()

    @pl.loop(0, TOK // ROWS)
    def _(r):
        at = pl.ds(pl.multiple_of(r * ROWS, ROWS), ROWS)
        total = mm(cot[at, :], weight[:, heads.columns(heads.y)], NT)
        for other in heads.others:
            total += mm(parts_in[other, at, :], weight[:, heads.columns(other)], NT)
        tokens[at, :] = total.astype(jnp.bfloat16)

    for other in heads.others:
        pl.semaphore_signal(ready, inc=1, device_id={"head": other}, device_id_type=MESH)

    each("A", range(8, 12))
    each("B", range(8, 12))
    step("CD", 8)
    step("H", 5)
    step("E", 7)
    step("CD", 9)
    step("G", 6)
    step("H", 6)
    step("F", 7)
    step("CD", 10)
    step("CD", 11)
    step("G", 7)
    step("H", 7)

    @pl.loop(0, HD)
    def _(h):
        head_forward(h, x_u, v_u, bias, att_u, attt, lse, s_ref, p_ref)

    each("A", range(12, 16))
    each("B", range(12, 15))
    step("E", 8)
    step("F", 8)
    step("C", 12)
    step("B", 15)
    step("D", 12)
    step("E", 9)
    step("F", 9)
    step("G", 8)
    step("CD", 13)
    step("H", 8)
    step("E", 10)
    step("F", 10)
    step("G", 9)
    step("CD", 14)
    step("H", 9)
    step("E", 11)
    step("F", 11)
    step("G", 10)
    step("CD", 15)
    step("H", 10)
    step("G", 11)
    step("H", 11)

    @pl.loop(0, HD)
    def _(h):
        head_backward(h, x_u, v_u, g_u, bias, attt, lse, gx_u, gv_u, acc, acct)

    each("A", range(16, 20))
    each("B", range(16, 18))
    step("E", 12)
    step("F", 12)
    step("E", 13)
    step("F", 13)
    step("G", 12)
    each("B", range(18, 20))
    step("CD", 16)
    step("H", 12)
    step("E", 14)
    step("F", 14)
    step("G", 13)
    step("CD", 17)
    step("H", 13)
    step("E", 15)
    step("F", 15)
    step("CD", 18)
    step("G", 14)
    step("CD", 19)
    step("A", 20)
    sums = [heads.copy(2, d, parts_out.at[d], parts_in.at[heads.y]) for d in range(3)]
    for t in range(16, 26):
        step("H", t - 2)
        step("E", t)
        step("D", t + 2 if t >= 18 else -1)
        step("C", t + 3 if t >= 17 else -1)
        step("B", t + 4)
        step("A", t + 5)
        step("F", t)
        step("G", t - 1)
        if t == 17:
            pl.semaphore_wait(ready, 3)
            for d in (1, 0, 2):

                @pl.loop(0, TOK // ROWS)
                def _(r):
                    at = pl.ds(pl.multiple_of(r * ROWS, ROWS), ROWS)
                    part = mm(tokens[at, :], weight[:, heads.columns(heads.others[d])])
                    parts_out[d, at, :] = part.astype(jnp.bfloat16)

                sums[d].start()

            @pl.loop(0, TOK // ROWS)
            def _(r):
                at = pl.ds(pl.multiple_of(r * ROWS, ROWS), ROWS)
                output[at, :] = mm(tokens[at, :], weight[:, heads.columns(heads.y)]).astype(jnp.bfloat16)

    for cp in flag_cps + sums:
        cp.wait()
    any_flag[...] = jnp.max(flags[...], axis=0)

    @pl.loop(0, TOK // ROWS)
    def _(r):
        at = pl.ds(pl.multiple_of(r * ROWS, ROWS), ROWS)
        total = output[at, :].astype(jnp.float32)
        for other in heads.others:
            total += parts_in[other, at, :].astype(jnp.float32)
        output[at, :] = total.astype(jnp.bfloat16)


def layer(tables, flag, qk, values, cot, weight, bias, caps, cid):
    vmem = pl.BlockSpec(memory_space=pltpu.VMEM)
    units = pltpu.VMEM((ITEMS, BLOCK, BLOCK), jnp.bfloat16)
    tokens = pltpu.VMEM((TOK, WIDTH), jnp.bfloat16)
    scratch = list(FORWARD_SCRATCH + BACKWARD_SCRATCH) + [units] * 5 + [tokens]
    scratch += [
        pltpu.VMEM((4, TOK, WIDTH), jnp.bfloat16),
        pltpu.VMEM((3, TOK, WIDTH), jnp.bfloat16),
        pltpu.VMEM((4, 8, BLOCK), jnp.float32),
        pltpu.SemaphoreType.DMA((3, 3)),
        pltpu.SemaphoreType.DMA((3, 3)),
        pltpu.SemaphoreType.REGULAR,
    ]
    return pl.pallas_call(
        functools.partial(layer_kernel, caps),
        out_shape=[TOKENS] * 3 + [jax.ShapeDtypeStruct((8, BLOCK), jnp.float32)],
        in_specs=[pl.BlockSpec(memory_space=pltpu.SMEM)] + [vmem] * 6,
        out_specs=[vmem] * 4,
        scratch_shapes=scratch + link_scratch(SETS, CHUNKS, *caps),
        compiler_params=pltpu.CompilerParams(
            collective_id=cid, has_side_effects=True, vmem_limit_bytes=VMEM_BYTES
        ),
    )(tables, flag, qk, values, cot, weight, bias)


def attention_kernel(x_ref, v_ref, g_ref, bias_ref, att, gx_ref, gv_ref, attt, lse, s_ref, p_ref, acc, acct):
    @pl.loop(0, HD)
    def _(h):
        head_forward(h, x_ref, v_ref, bias_ref, att, attt, lse, s_ref, p_ref)
        head_backward(h, x_ref, v_ref, g_ref, bias_ref, attt, lse, gx_ref, gv_ref, acc, acct)


def attention(x, v, g, bias):
    vmem = pl.BlockSpec(memory_space=pltpu.VMEM)
    return pl.pallas_call(
        attention_kernel,
        out_shape=[UNITS] * 3,
        in_specs=[vmem] * 4,
        out_specs=[vmem] * 3,
        scratch_shapes=list(FORWARD_SCRATCH + BACKWARD_SCRATCH),
        compiler_params=pltpu.CompilerParams(vmem_limit_bytes=VMEM_BYTES),
    )(x, v, g, bias)


def model_output(attended, out_weight):
    partial_term = jnp.dot(attended, out_weight, preferred_element_type=jnp.float32)
    return lax.psum_scatter(partial_term.astype(jnp.bfloat16), "head", scatter_dimension=1, tiled=True)


def cotangent_heads(out_cotangent, out_weight):
    gathered = lax.all_gather(out_cotangent, "head", axis=1, tiled=True)
    return jnp.einsum("tn,kn->tk", gathered, out_weight, preferred_element_type=jnp.float32).astype(
        jnp.bfloat16
    )


def per_device(qk, values, out_weight, out_cotangent, cluster_ids):
    tables, bias, flag = fast_routing(cluster_ids, FAST)
    *fast, any_lost = layer(tables, flag, qk, values, out_cotangent, out_weight, bias, FAST, 0)

    def slow(args):
        me = lax.axis_index("seq").astype(I32)
        place = choose_places((cluster_ids // CL_OWN).reshape(N_SEQ, ITEMS))
        tables, bias, _ = routing(me, cluster_ids, place, *FULL)
        tables = tables[None]
        grad_attended = cotangent_heads(out_cotangent, out_weight)
        sources = jnp.stack([qk, values, grad_attended])
        x, v, g = lax.map(lambda a: exchange(tables, a, True, FULL, 1), sources)
        units = jnp.stack(attention(x, v, g, bias))
        home = lax.map(lambda a: exchange(tables, a, False, FULL, 2), units)
        return [model_output(home[0], out_weight), home[1], home[2]]

    return tuple(lax.cond(any_lost[0, 0] > 0, slow, lambda args: args, fast))


def solution(mesh):
    return jax.shard_map(
        per_device,
        mesh=mesh,
        in_specs=(
            P("seq", "head"),
            P("seq", "head"),
            P("head", None),
            P("seq", "head"),
            P(None, "head"),
        ),
        out_specs=(P("seq", "head"), P("seq", "head"), P("seq", "head")),
        check_vma=False,
    )
```
